128 devices in a mesh: seq: 32 (over z_lo, y, x), fsdp: 4 (over z_hi, core).
Axes of the slice: x: 4, y: 4, z: 4 (z_hi: 2, z_lo: 2; z = z_hi * 2 + z_lo), core: 2. Of those that a mesh axis runs over, the one named last changes fastest.
Arguments:
- tokens: bfloat16 [4, 8192, 2048], P('fsdp', 'seq'), may hold values from -6 to 6
- w_in: bfloat16 [2048, 2304], P('fsdp'), may hold values from -0.125 to 0.125
- log_decay: float32 [4, 32, 8192], P('fsdp', None, 'seq'), may hold values from -2 to 0, as said below
- grad_out: bfloat16 [4, 8192, 2048], P('fsdp', 'seq'), may hold values from -6 to 6
Outputs:
- mixer_out: bfloat16 [4, 8192, 2048], P('fsdp', 'seq')
- grad_tokens: bfloat16 [4, 8192, 2048], P('fsdp', 'seq')
- grad_weights: float32 [2048, 2304], P(('seq', 'fsdp'))
The draws below stay inside these ranges and needn't reach their ends.
Inputs may be any that keep to these rules, and one draw needn't show every extreme that they name: `log_decay`: each entry is the logarithm of a decay factor below one.
All inputs are finite; a program needn't handle non-finite values.
Results may differ from the reference program's by a relative error of at most 0.015.
Values may be sent and summed in bfloat16 or wider, within the bound.
A program may use at most 192 MiB of HBM per device.

```python
import math
import jax
import jax.numpy as jnp
from jax import lax

D = 2048
H = 32
P_SIZE = 64
N = 128
BLOCK = 256
TOK_DEV = 256
LENGTH = 8192
SEQS = 4
COLS = 2304


def draw_log_decay(key, part):
    streams = jax.random.split(key, 7)
    fast_share = 0.5
    slow_rate = jnp.exp(jax.random.uniform(streams[1], (SEQS, H, 1), minval=math.log(0.05), maxval=math.log(0.3))) / LENGTH
    fast_heads = jax.random.bernoulli(streams[0], fast_share, (SEQS, H, 1))
    fast_rate = jnp.exp(jax.random.uniform(streams[2], (SEQS, H, 1), minval=math.log(1.0 / 50.0), maxval=math.log(1.0 / 30.0)))
    head_rate = jnp.where(fast_heads, fast_rate, slow_rate)
    spans = LENGTH // TOK_DEV
    device_factor = jnp.exp(jax.random.uniform(streams[3], (SEQS, H, spans, 1), minval=-math.log(2.0), maxval=math.log(2.0)))
    device_factor = jnp.broadcast_to(device_factor, (SEQS, H, spans, TOK_DEV)).reshape(SEQS, H, LENGTH)
    roughness = jax.random.uniform(streams[4], (SEQS, H, LENGTH), minval=0.7, maxval=1.4)
    final_output = -head_rate * device_factor * roughness
    token_places = jax.random.randint(streams[5], (SEQS, 2), 0, LENGTH)
    dropped_tokens = jnp.log(jax.random.uniform(streams[6], (SEQS, H, 2), minval=0.55, maxval=0.8))
    token_position = lax.broadcasted_iota(jnp.int32, (SEQS, 1, LENGTH), 2)
    for spike_amount in range(2):
        matched_entry = token_position == token_places[:, spike_amount][:, None, None]
        final_output = final_output + jnp.where(matched_entry, dropped_tokens[:, :, spike_amount][:, :, None], 0.0)
    return final_output.astype(jnp.float32)


def strengthened(values, stream_key, source, target, shards_of, factor):
    owner, partner = [(jnp.arange(values.shape[axis_at]) // (values.shape[axis_at] // shards_of)).reshape([-1 if axis == axis_at else 1 for axis in range(values.ndim)]) for axis_at in (source, target)]
    chosen = jax.random.permutation(stream_key, shards_of)[partner]
    strong = (owner == chosen) | (owner == (partner + shards_of // 2) % shards_of)
    return jnp.where(strong, factor * values, values)


def block_levels(rng, shape, shards, low, largest):
    gain = 1.0
    for dim, parts in shards:
        draws = jax.random.uniform(jax.random.fold_in(jax.random.fold_in(rng, 6), dim), (parts,), jnp.float32, low / len(shards), largest / len(shards))
        gain = gain * jnp.repeat(jnp.exp(draws), shape[dim] // parts).reshape((-1,) + (1,) * (len(shape) - 1 - dim))
    return gain


def bell_draw(rng, shape, deviation, reach, cuts=(), kind=jnp.bfloat16):
    loudness = block_levels(rng, shape, cuts, -0.22, 0.18) if cuts else 1.0
    result = jax.random.normal(rng, shape, jnp.float32) * deviation * loudness
    return jnp.minimum(jnp.maximum(result, -reach), reach).astype(kind)


def noise_with(stream_key, dims, width, reach, cuts, heavy, dtype=jnp.bfloat16):
    result = width * jax.random.normal(stream_key, dims, jnp.float32)
    if cuts:
        result = result * block_levels(stream_key, dims, cuts, -0.22, 0.18)
    return jnp.clip(strengthened(result, jax.random.fold_in(stream_key, 3), *heavy), -reach, reach).astype(dtype)


def setup_inputs(seed: int = 0) -> dict:
    keys = jax.random.split(jax.random.key(seed), 5)
    return {
        "tokens": noise_with(keys[0], (SEQS, LENGTH, D), 1.0, 6.0, ((0, 4), (1, 32)), (1, 2, 32, 2.75)),
        "w_in": bell_draw(keys[1], (D, COLS), D ** -0.5, 0.125, ((0, 4),)),
        "log_decay": draw_log_decay(jax.random.fold_in(keys[4], 71), 0),
        "grad_out": bell_draw(keys[3], (SEQS, LENGTH, H * P_SIZE), 1.0, 6.0, ((0, 4), (1, 32))),
    }


highest = lax.Precision.HIGHEST
epsilon = 1e-05

def block_chain(log_rates, terms, backward, start_state):

    def advance(carried, packed):
        log_k, term_k = packed
        return (jnp.exp(log_k)[:, None, None] * carried + term_k, carried)
    finish, inputs = lax.scan(advance, start_state, (log_rates, terms), reverse=backward)
    return (inputs, finish)

def decay_matrix(cumulative, log_rates):
    extent = cumulative.shape[-1]
    row_idx = lax.broadcasted_iota(jnp.int32, (extent, extent), 0)
    col_idx = lax.broadcasted_iota(jnp.int32, (extent, extent), 1)
    later_gap = cumulative[:, :, None] - cumulative[:, None, :]
    exclusive = cumulative - log_rates
    earlier_gap = exclusive[:, None, :] - exclusive[:, :, None]
    exponent = jnp.where(row_idx > col_idx, later_gap, jnp.where(row_idx < col_idx, earlier_gap, 0.0))
    return jnp.exp(exponent) + (row_idx == col_idx).astype(jnp.float32)

def mix_sequence(xbc_float, log_rates):
    block_count = LENGTH // BLOCK
    inner_width = H * P_SIZE
    values = xbc_float[:, :inner_width].reshape(block_count, BLOCK, H, P_SIZE)
    key_rows = xbc_float[:, inner_width:inner_width + N].reshape(block_count, BLOCK, N)
    queries = xbc_float[:, inner_width + N:].reshape(block_count, BLOCK, N)
    blocked = log_rates.reshape(H, block_count, BLOCK).transpose(1, 0, 2)
    cumulative = jnp.cumsum(blocked, axis=-1)
    totals = cumulative[:, :, -1]
    to_end = jnp.exp(totals[:, :, None] - cumulative)
    from_start = jnp.exp(cumulative - blocked)
    end_terms = jnp.einsum('khq,kqhp,kqn->khpn', to_end, values, key_rows, precision=highest)
    start_terms = jnp.einsum('khq,kqhp,kqn->khpn', from_start, values, key_rows, precision=highest)
    zero_state = jnp.zeros((H, P_SIZE, N), jnp.float32)
    fwd_in, _ = block_chain(totals, end_terms, False, zero_state)
    rev_next, _ = block_chain(totals, start_terms, True, zero_state)

    def block_values(packed):
        block_vals, block_keys, block_queries, block_cumul, block_logs, block_total, state_in, state_next = packed
        affinity = jnp.dot(block_queries, block_keys.T, precision=highest)
        weighted = affinity[None] * decay_matrix(block_cumul, block_logs)
        inner_part = jnp.einsum('hij,jhp->ihp', weighted, block_vals, precision=highest)
        enter_weight = jnp.exp(block_cumul).T[:, :, None]
        leave_weight = jnp.exp(block_total[:, None] - (block_cumul - block_logs)).T[:, :, None]
        carried_in = jnp.einsum('qn,hpn->qhp', block_queries, state_in, precision=highest) * enter_weight
        carried_back = jnp.einsum('qn,hpn->qhp', block_queries, state_next, precision=highest) * leave_weight
        return inner_part + carried_in + carried_back
    mixture = lax.map(jax.checkpoint(block_values), (values, key_rows, queries, cumulative, blocked, totals, fwd_in, rev_next))
    row_scale = jnp.sqrt(lax.optimization_barrier(jnp.mean(mixture * mixture, axis=-1)) + epsilon)
    normed = mixture / row_scale[..., None]
    return normed.reshape(LENGTH, H * P_SIZE)

def forward_pass(xbc_rows, log_rates):
    return mix_sequence(xbc_rows.astype(jnp.float32), log_rates).astype(jnp.bfloat16)

def reference(tokens, w_in, log_decay, grad_out):
    flat_tokens = tokens.reshape(SEQS * LENGTH, D)
    xbc_rows = jnp.dot(flat_tokens, w_in, preferred_element_type=jnp.float32).astype(jnp.bfloat16)
    xbc_rows = lax.optimization_barrier(xbc_rows).reshape(SEQS, LENGTH, COLS)

    def per_sequence(packed):
        seq_rows, seq_logs, seq_grad = packed
        outputs, pullback = jax.vjp(lambda inputs: forward_pass(inputs, seq_logs), seq_rows)
        return (outputs, pullback(seq_grad)[0])
    mixer_out, grad_proj = lax.map(per_sequence, (xbc_rows, log_decay, grad_out))
    flat_grad = grad_proj.reshape(SEQS * LENGTH, COLS)
    grad_tokens = jnp.dot(flat_grad, w_in.T, preferred_element_type=jnp.float32).astype(jnp.bfloat16)
    grad_weights = jnp.dot(flat_tokens.T, flat_grad, preferred_element_type=jnp.float32)
    return (mixer_out, grad_tokens.reshape(SEQS, LENGTH, D), grad_weights)
```

```python
import functools
import jax
import jax.numpy as jnp
from jax import lax
from jax.experimental import pallas as pl
from jax.experimental.pallas import tpu as pltpu
from jax.sharding import PartitionSpec as P

BF = jnp.bfloat16
F32 = jnp.float32
EPS = 1e-5
H, PS, N, T, D, INNER, COLS = 32, 64, 128, 256, 2048, 2048, 2304
MESH = pl.DeviceIdType.MESH
NN = (((1,), (0,)), ((), ()))
NT = (((1,), (1,)), ((), ()))
TN = (((0,), (0,)), ((), ()))


def mm(a, b, dims):
    return lax.dot_general(a, b, dims, preferred_element_type=F32)


def place():
    s = lax.axis_index("seq")
    f = lax.axis_index("fsdp")
    return s % 4, (s // 4) % 4, s // 16, f // 2, f % 2


def device(x, y, zl, zh, core):
    return (zl * 16 + y * 4 + x, zh * 2 + core)


def flip(dim, x, y, zl, zh):
    if dim == 0:
        x = x + 1 - 2 * (x % 2)
    elif dim == 1:
        x = 3 - x
    elif dim == 2:
        y = y + 1 - 2 * (y % 2)
    elif dim == 3:
        y = 3 - y
    elif dim == 4:
        zl = 1 - zl
    else:
        zl, zh = 1 - zl, 1 - zh
    return x, y, zl, zh


def greet(peers):
    barrier = pltpu.get_barrier_semaphore()
    for peer in peers:
        pl.semaphore_signal(barrier, inc=1, device_id=peer, device_id_type=MESH)
    pl.semaphore_wait(barrier, len(peers))


def gather_kernel(w_ref, out_ref, send, recv, local):
    x, y, zl, zh, core = place()
    f = zh * 2 + core
    far_f = (1 - zh) * 2 + core
    sib = device(x, y, zl, zh, 1 - core)
    far = device(*flip(5, x, y, zl, zh), core)
    greet([sib, far])
    parts = 4
    rows = 512 // parts
    own = pltpu.make_async_copy(w_ref, out_ref.at[pl.ds(pl.multiple_of(f * 512, 512), 512)], local)
    own.start()
    started = []
    over = []
    for i in range(parts):
        here = pl.ds(i * rows, rows)
        there = pl.ds(pl.multiple_of(f * 512 + i * rows, rows), rows)
        c = pltpu.make_async_remote_copy(
            w_ref.at[here], out_ref.at[there], send.at[0, i], recv.at[0, i], far, MESH
        )
        c.start()
        over.append(c)
    for i in range(parts):
        here = pl.ds(i * rows, rows)
        there = pl.ds(pl.multiple_of(f * 512 + i * rows, rows), rows)
        c = pltpu.make_async_remote_copy(
            w_ref.at[here], out_ref.at[there], send.at[1, i], recv.at[1, i], sib, MESH
        )
        c.start()
        started.append(c)
    for i in range(parts):
        there = pl.ds(pl.multiple_of(far_f * 512 + i * rows, rows), rows)
        over[i].wait_recv()
        c = pltpu.make_async_remote_copy(
            out_ref.at[there], out_ref.at[there], send.at[2, i], recv.at[2, i], sib, MESH
        )
        c.start()
        started.append(c)
    for c in started:
        c.wait()
    for c in over:
        c.wait_send()
    own.wait()


def gather_weight(w):
    return pl.pallas_call(
        gather_kernel,
        name="gather_weight",
        out_shape=jax.ShapeDtypeStruct((D, COLS), BF),
        in_specs=[pl.BlockSpec(memory_space=pltpu.VMEM)],
        out_specs=pl.BlockSpec(memory_space=pltpu.VMEM),
        scratch_shapes=[
            pltpu.SemaphoreType.DMA((3, 4)),
            pltpu.SemaphoreType.DMA((3, 4)),
            pltpu.SemaphoreType.DMA,
        ],
        compiler_params=pltpu.CompilerParams(
            collective_id=0, has_side_effects=True, vmem_limit_bytes=40 << 20
        ),
    )(w)


def mixer_kernel(
    xt_ref, gt_ref, rows_ref, cum_ref, cumt_ref, exc_ref, exct_ref, tot_ref,
    out_ref, grad_ref,
    dec, aff, y, gm, gmw, xs, gaff, dct, dbt, bmat, cmat,
    up1, in1, down1, ent, up2, in2, down2, adj, tin,
    ssem, rsem, tsem, trsem,
):
    s = lax.axis_index("seq")
    f = lax.axis_index("fsdp")
    barrier = pltpu.get_barrier_semaphore()

    def peer(o):
        return lax.rem(s + o, 32)

    @pl.loop(1, 32)
    def _(o):
        pl.semaphore_signal(barrier, inc=1, device_id=(peer(o), f), device_id_type=MESH)

    ri = lax.broadcasted_iota(jnp.int32, (T, T), 0)
    ci = lax.broadcasted_iota(jnp.int32, (T, T), 1)
    diag = ri == ci
    for h in range(H):
        a = cum_ref[h : h + 1, :] - cumt_ref[:, h : h + 1]
        b = exct_ref[:, h : h + 1] - exc_ref[h : h + 1, :]
        e = jnp.exp(jnp.minimum(a, b))
        dec[h] = jnp.where(diag, 2.0, e).astype(BF)

    bt = xt_ref[pl.ds(INNER, N), :]
    ct = xt_ref[pl.ds(INNER + N, N), :]
    bmat[...] = bt.T
    cmat[...] = ct.T

    def head(h):
        return pl.ds(pl.multiple_of(h * PS, PS), PS)

    @pl.loop(0, H)
    def _(h):
        xv = xt_ref[head(h), :].astype(F32)
        r = rows_ref[h]
        w0 = (xv * r[2:3, :]).astype(BF)
        w1 = (xv * r[3:4, :]).astype(BF)
        xs[h, pl.ds(0, PS), :] = w1
        xs[h, pl.ds(PS, PS), :] = w0
        up1[h, pl.ds(0, PS), :] = mm(w0, bmat[...], NN).astype(BF)
        up1[h, pl.ds(PS, PS), :] = mm(w1, bmat[...], NN).astype(BF)

    pl.semaphore_wait(barrier, 31)

    def tots(o):
        p = peer(o)
        return pltpu.make_async_remote_copy(
            tot_ref.at[p], tin.at[s], tsem.at[p], trsem.at[s], (p, f), MESH
        )

    def sending(k, src, dst, o):
        p = peer(o)
        return pltpu.make_async_remote_copy(
            src.at[p], dst.at[s], ssem.at[k, p], rsem.at[k, s], (p, f), MESH
        )

    def arriving(k, src, dst, o):
        p = peer(o)
        return pltpu.make_async_remote_copy(
            src.at[p], dst.at[p], ssem.at[k, p], rsem.at[k, p], (p, f), MESH
        )

    @pl.loop(1, 32)
    def _(o):
        tots(o).start()
        sending(0, up1, in1, o).start()

    tin[s] = tot_ref[s]
    in1[s] = up1[s]

    aff[...] = mm(bmat[...], ct, NN).astype(BF)

    @pl.loop(0, H)
    def _(h):
        wt = aff[...] * dec[h]
        y[h] = mm(xt_ref[head(h), :], wt, NN)

    @pl.loop(1, 32)
    def _(o):
        p = peer(o)
        pltpu.make_async_remote_copy(
            tot_ref.at[p], tin.at[p], tsem.at[p], trsem.at[p], (p, f), MESH
        ).wait_recv()
        arriving(0, up1, in1, o).wait_recv()

    def scan(src, dst):
        def one(i, state):
            fwd, rev = state
            k = 31 - i
            dst[i, pl.ds(0, PS), :] = fwd.astype(BF)
            dst[k, pl.ds(PS, PS), :] = rev.astype(BF)
            fwd = jnp.exp(tin[i][0:1, :]) * fwd + src[i, pl.ds(0, PS), :].astype(F32)
            rev = jnp.exp(tin[k][0:1, :]) * rev + src[k, pl.ds(PS, PS), :].astype(F32)
            return fwd, rev

        zero = jnp.zeros((PS, N), F32)
        lax.fori_loop(0, 32, one, (zero, zero))

    scan(in1, down1)

    @pl.loop(1, 32)
    def _(o):
        sending(1, down1, ent, o).start()

    ent[s] = down1[s]

    @pl.loop(1, 32)
    def _(o):
        arriving(1, down1, ent, o).wait_recv()

    @pl.loop(0, H)
    def _(h):
        r = rows_ref[h]
        car = mm(ent[h], xt_ref[pl.ds(INNER + N, N), :], NN)
        mix = y[h] + r[0:1, :] * car[:PS] + r[1:2, :] * car[PS:]
        ms = jnp.sum(mix * mix, axis=0, keepdims=True) * (1.0 / PS)
        inv = 1.0 / jnp.sqrt(ms + EPS)
        z = mix * inv
        out_ref[head(h), :] = z.astype(BF)
        gv = gt_ref[head(h), :].astype(F32)
        m = jnp.sum(gv * z, axis=0, keepdims=True) * (1.0 / PS)
        gr = (gv - z * m) * inv
        gm[h] = gr.astype(BF)
        g0 = (gr * r[0:1, :]).astype(BF)
        g1 = (gr * r[1:2, :]).astype(BF)
        gmw[h, pl.ds(0, PS), :] = g0
        gmw[h, pl.ds(PS, PS), :] = g1
        up2[h, pl.ds(0, PS), :] = mm(g1, cmat[...], NN).astype(BF)
        up2[h, pl.ds(PS, PS), :] = mm(g0, cmat[...], NN).astype(BF)

    @pl.loop(1, 32)
    def _(o):
        sending(2, up2, in2, o).start()

    in2[s] = up2[s]

    gaff[...] = jnp.zeros_like(gaff)
    dct[...] = jnp.zeros_like(dct)
    dbt[...] = jnp.zeros_like(dbt)

    @pl.loop(0, H)
    def _(h):
        d = dec[h]
        wt = aff[...] * d
        g = gm[h]
        y[h] = mm(g, wt, NT)
        gw = mm(xt_ref[head(h), :], g, TN)
        gaff[...] += gw * d.astype(F32)
        dct[...] += mm(ent[h], gmw[h], TN)

    @pl.loop(1, 32)
    def _(o):
        arriving(2, up2, in2, o).wait_recv()

    scan(in2, down2)

    @pl.loop(1, 32)
    def _(o):
        sending(3, down2, adj, o).start()

    adj[s] = down2[s]
    ga = gaff[...].astype(BF)
    dct[...] += mm(xt_ref[pl.ds(INNER, N), :], ga, NN)
    dbt[...] += mm(xt_ref[pl.ds(INNER + N, N), :], ga, NT)

    @pl.loop(1, 32)
    def _(o):
        arriving(3, down2, adj, o).wait_recv()

    @pl.loop(0, H)
    def _(h):
        r = rows_ref[h]
        car = mm(adj[h], xt_ref[pl.ds(INNER, N), :], NN)
        gx = y[h] + r[3:4, :] * car[:PS] + r[2:3, :] * car[PS:]
        grad_ref[head(h), :] = gx.astype(BF)
        dbt[...] += mm(adj[h], xs[h], TN)

    grad_ref[pl.ds(INNER, N), :] = dbt[...].astype(BF)
    grad_ref[pl.ds(INNER + N, N), :] = dct[...].astype(BF)

    @pl.loop(1, 32)
    def _(o):
        tots(o).wait_send()
        sending(0, up1, in1, o).wait_send()
        sending(1, down1, ent, o).wait_send()
        sending(2, up2, in2, o).wait_send()
        sending(3, down2, adj, o).wait_send()


def mixer(xbct, gt, log):
    cum = jnp.cumsum(log, axis=1)
    exc = cum - log
    tot = cum[:, -1:]
    rows = jnp.stack(
        [jnp.exp(cum), jnp.exp(tot - exc), jnp.exp(tot - cum), jnp.exp(exc)] + [exc] * 4, axis=1
    )
    totb = jnp.broadcast_to(tot[:, :, None], (H, 8, 128))
    v = pl.BlockSpec(memory_space=pltpu.VMEM)
    st = pltpu.VMEM((H, 2 * PS, N), BF)
    return pl.pallas_call(
        mixer_kernel,
        name="mixer",
        out_shape=(
            jax.ShapeDtypeStruct((INNER, T), BF),
            jax.ShapeDtypeStruct((COLS, T), BF),
        ),
        in_specs=[v] * 8,
        out_specs=(v, v),
        scratch_shapes=[
            pltpu.VMEM((H, T, T), BF),
            pltpu.VMEM((T, T), BF),
            pltpu.VMEM((H, PS, T), F32),
            pltpu.VMEM((H, PS, T), BF),
            pltpu.VMEM((H, 2 * PS, T), BF),
            pltpu.VMEM((H, 2 * PS, T), BF),
            pltpu.VMEM((T, T), F32),
            pltpu.VMEM((N, T), F32),
            pltpu.VMEM((N, T), F32),
            pltpu.VMEM((T, N), BF),
            pltpu.VMEM((T, N), BF),
            st, st, st, st, st, st, st, st,
            pltpu.VMEM((H, 8, 128), F32),
            pltpu.SemaphoreType.DMA((4, 32)),
            pltpu.SemaphoreType.DMA((4, 32)),
            pltpu.SemaphoreType.DMA((32,)),
            pltpu.SemaphoreType.DMA((32,)),
        ],
        compiler_params=pltpu.CompilerParams(
            collective_id=1, has_side_effects=True, vmem_limit_bytes=56 << 20
        ),
    )(xbct, gt, rows, cum, cum.T, exc, exc.T, totb)


CW = COLS // 6
OFF = [0, 32, 48, 56, 60, 62]


def order(color):
    dims = [(color + k) % 6 for k in range(6)]
    found = []
    for i in range(64):
        r = 0
        for k in range(6):
            if (i >> (5 - k)) & 1:
                r |= 1 << dims[k]
        found.append(r)
    return found


def wgrad_kernel(tok_ref, g_ref, out_ref, ta, tb, ts, gs, acc, sb, rb, ssem, rsem, xs, xr):
    x, y, zl, zh, core = place()
    sib = device(x, y, zl, zh, 1 - core)
    peers = [device(*flip(d, x, y, zl, zh), core) for d in range(6)]
    greet(peers + [sib])
    c0 = pltpu.make_async_remote_copy(g_ref, gs, xs.at[0], xr.at[0], sib, MESH)
    c1 = pltpu.make_async_remote_copy(tok_ref.at[1 - core], ts, xs.at[1], xr.at[1], sib, MESH)
    c1.start()
    c0.start()

    def block(r):
        p = (x, y, zl, zh)
        for d in range(6):
            if (r >> d) & 1:
                p = flip(d, *p)
        return p[2] * 32 + p[1] * 8 + p[0] * 2 + p[3]

    for r in range(64):
        ta[r] = tok_ref[core, block(r)]
    c1.wait_recv()
    for r in range(64):
        tb[r] = ts[block(r)]
    c0.wait_recv()

    def product(c, half):
        ids = order(c)[32 * half : 32 * half + 32]
        la = jnp.concatenate([ta[r] for r in ids], axis=0)
        lb = jnp.concatenate([tb[r] for r in ids], axis=0)
        cols = pl.ds(c * CW, CW)
        return (mm(la, g_ref[:, cols], NN) + mm(lb, gs[:, cols], NN)).reshape(32, 16, CW)

    def copy(c, k):
        n = 32 >> k
        part = pl.ds(OFF[k], n)
        return pltpu.make_async_remote_copy(
            sb.at[c, part], rb.at[c, part], ssem.at[c, k], rsem.at[c, k], peers[(c + k) % 6], MESH
        )

    for c in range(6):
        sb[c, pl.ds(0, 32)] = product(c, 1).astype(BF)
        copy(c, 0).start()
    for c in range(6):
        acc[c] = product(c, 0)
    for k in range(1, 6):
        n = 64 >> k
        m = n // 2
        for c in range(6):
            copy(c, k - 1).wait_recv()
            hi = acc[c, pl.ds(m, m)] + rb[c, pl.ds(OFF[k - 1] + m, m)].astype(F32)
            sb[c, pl.ds(OFF[k], m)] = hi.astype(BF)
            copy(c, k).start()
        for c in range(6):
            acc[c, pl.ds(0, m)] += rb[c, pl.ds(OFF[k - 1], m)].astype(F32)
    for c in range(6):
        copy(c, 5).wait_recv()
        out_ref[:, pl.ds(c * CW, CW)] = acc[c, 0] + rb[c, OFF[5]].astype(F32)
    for c in range(6):
        for k in range(6):
            copy(c, k).wait_send()
    c0.wait_send()
    c1.wait_send()


def weight_gradient(tokt, g):
    v = pl.BlockSpec(memory_space=pltpu.VMEM)
    return pl.pallas_call(
        wgrad_kernel,
        name="weight_gradient",
        out_shape=jax.ShapeDtypeStruct((16, COLS), F32),
        in_specs=[v, v],
        out_specs=v,
        scratch_shapes=[
            pltpu.VMEM((64, 16, T), BF),
            pltpu.VMEM((64, 16, T), BF),
            pltpu.VMEM((64, 16, T), BF),
            pltpu.VMEM((T, COLS), BF),
            pltpu.VMEM((6, 32, 16, CW), F32),
            pltpu.VMEM((6, 63, 16, CW), BF),
            pltpu.VMEM((6, 63, 16, CW), BF),
            pltpu.SemaphoreType.DMA((6, 6)),
            pltpu.SemaphoreType.DMA((6, 6)),
            pltpu.SemaphoreType.DMA((2,)),
            pltpu.SemaphoreType.DMA((2,)),
        ],
        compiler_params=pltpu.CompilerParams(
            collective_id=2, has_side_effects=True, vmem_limit_bytes=48 << 20
        ),
    )(tokt, g)


def on_device(tokens, w_in, log_decay, grad_out):
    tok = tokens[0]
    w = gather_weight(w_in)
    xbct = mm(w, tok, (((0,), (1,)), ((), ()))).astype(BF)
    tokt = tok.T.reshape(64, 2, 16, T).transpose(1, 0, 2, 3)
    outt, gradt = mixer(xbct, grad_out[0].T, log_decay[0])
    g = gradt.T
    grad_w = weight_gradient(tokt, g)
    grad_tokens = mm(g, w, NT).astype(BF)
    return outt.T[None], grad_tokens[None], grad_w


def solution(mesh):
    return jax.shard_map(
        on_device,
        mesh=mesh,
        in_specs=(
            P("fsdp", "seq", None),
            P("fsdp", None),
            P("fsdp", None, "seq"),
            P("fsdp", "seq", None),
        ),
        out_specs=(P("fsdp", "seq", None), P("fsdp", "seq", None), P(("seq", "fsdp"), None)),
        check_vma=False,
    )
```

```python
import functools
import jax
import jax.numpy as jnp
from jax import lax
from jax.experimental import pallas as pl
from jax.experimental.pallas import tpu as pltpu
from jax.sharding import PartitionSpec as P

BF = jnp.bfloat16
F32 = jnp.float32
EPS = 1e-5
H, PS, N, T, D, INNER, COLS = 32, 64, 128, 256, 2048, 2048, 2304
MESH = pl.DeviceIdType.MESH
NN = (((1,), (0,)), ((), ()))
NT = (((1,), (1,)), ((), ()))
TN = (((0,), (0,)), ((), ()))
CW = COLS // 6
OFF = [0, 32, 48, 56, 60, 62]
SUB = 4
ROWS = 128 // SUB


def mm(a, b, dims):
    return lax.dot_general(a, b, dims, preferred_element_type=F32)


def place():
    s = lax.axis_index("seq")
    f = lax.axis_index("fsdp")
    return s % 4, (s // 4) % 4, s // 16, f // 2, f % 2


def device(x, y, zl, zh, core):
    return (zl * 16 + y * 4 + x, zh * 2 + core)


def flip(dim, x, y, zl, zh):
    if dim == 0:
        x = x + 1 - 2 * (x % 2)
    elif dim == 1:
        x = 3 - x
    elif dim == 2:
        y = y + 1 - 2 * (y % 2)
    elif dim == 3:
        y = 3 - y
    elif dim == 4:
        zl = 1 - zl
    else:
        zl, zh = 1 - zl, 1 - zh
    return x, y, zl, zh


def order(color):
    dims = [(color + k) % 6 for k in range(6)]
    found = []
    for i in range(64):
        r = 0
        for k in range(6):
            if (i >> (5 - k)) & 1:
                r |= 1 << dims[k]
        found.append(r)
    return found


def remote(src, dst, ssem, rsem, to):
    return pltpu.make_async_remote_copy(src, dst, ssem, rsem, to, MESH)


def kernel(
    tok_hbm, w_hbm, log_ref, go_hbm,
    out_hbm, gt_hbm, gw_ref,
    wf, tok, tokt, ts, ta, tb, go, gtr, acc, xt, rows, tot, tin,
    dec, aff, y, gm, gmw, xs, gaff, dct, dbt, bmat, cmat,
    up1, in1, down1, ent, up2, in2, down2, adj,
    outt, outn, grad, g, gs, part, sb, rb,
    lsem, far_s, far_r, nb_s, nb_r, sf_s, sf_r, sib_s, sib_r,
    ssem, rsem, tsem, trsem, wsem, wrsem,
):
    s = lax.axis_index("seq")
    f = lax.axis_index("fsdp")
    x, y_, zl, zh, core = place()
    here = (x, y_, zl, zh)
    sib = device(*here, 1 - core)
    far = device(*flip(5, *here), core)
    peers = [device(*flip(d, *here), core) for d in range(6)]
    barrier = pltpu.get_barrier_semaphore()

    def peer(o, sign=1):
        px = lax.rem(x + 4 + sign * (o % 4), 4)
        py = lax.rem(y_ + 4 + sign * ((o // 4) % 4), 4)
        pz = lax.rem(zl + o // 16, 2)
        return pz * 16 + py * 4 + px

    @pl.loop(1, 32)
    def _(o):
        pl.semaphore_signal(barrier, inc=1, device_id=(peer(o), f), device_id_type=MESH)

    for q in (sib, far):
        pl.semaphore_signal(barrier, inc=1, device_id=q, device_id_type=MESH)

    def whole(i):
        return pl.ds(pl.multiple_of(i * 512, 512), 512)

    tok_in = pltpu.make_async_copy(tok_hbm, tok, lsem.at[0])
    go_in = pltpu.make_async_copy(go_hbm, go, lsem.at[1])
    own_in = pltpu.make_async_copy(w_hbm, wf.at[whole(f)], lsem.at[2])
    tok_in.start()
    own_in.start()
    go_in.start()

    ri = lax.broadcasted_iota(jnp.int32, (T, T), 0)
    ci = lax.broadcasted_iota(jnp.int32, (T, T), 1)
    log = log_ref[...]
    cum = lax.dot_general(
        log, (ri <= ci).astype(F32), NN, precision=lax.Precision.HIGHEST, preferred_element_type=F32
    )
    exc = cum - log
    last = cum[:, T - 1 : T]
    cumt = cum.T
    exct = exc.T
    fac = (jnp.exp(cum), jnp.exp(last - exc), jnp.exp(last - cum), jnp.exp(exc))
    lastb = jnp.broadcast_to(last, (H, N))
    for h in range(H):
        for k in range(4):
            rows[h, k : k + 1, :] = fac[k][h : h + 1, :]
        tot[h] = jnp.broadcast_to(lastb[h : h + 1, :], (8, N))

    pl.semaphore_wait(barrier, 33)

    far_f = (1 - zh) * 2 + core
    sibfar_f = (1 - zh) * 2 + 1 - core
    q0, q1 = (x + zl) % 2, (y_ + zl) % 2
    colour = q0 + 2 * q1
    others = [(1 - q0) + 2 * q1, q0 + 2 * (1 - q1), (1 - q0) + 2 * (1 - q1)]
    ndims = [0, 2, 4]

    def piece(shard, quarter, i):
        return pl.ds(pl.multiple_of(shard * 512 + quarter * 128 + i * ROWS, ROWS), ROWS)

    def far_copy(i):
        mine = pl.ds(pl.multiple_of(others[2] * 128 + i * ROWS, ROWS), ROWS)
        return remote(
            w_hbm.at[mine], wf.at[piece(f, others[2], i)], far_s.at[i], far_r.at[i], far
        )

    def near_copy(d, i):
        p = piece(far_f, colour, i)
        return remote(wf.at[p], wf.at[p], nb_s.at[d, i], nb_r.at[d, i], peers[ndims[d]])

    def pass_copy(j, i):
        p = piece(far_f, colour if j == 0 else others[j - 1], i)
        return remote(wf.at[p], wf.at[p], sf_s.at[j, i], sf_r.at[j, i], sib)

    own_out = remote(w_hbm, wf.at[whole(f)], sib_s.at[0], sib_r.at[0], sib)
    for i in range(SUB):
        far_copy(i).start()
    own_out.start()

    @pl.loop(1, 32)
    def _(o):
        p = peer(o)
        remote(tot.at[p], tin.at[s], tsem.at[p], trsem.at[s], (p, f)).start()

    tin[s] = tot[s]

    diag = ri == ci

    def decays(h):
        a = cum[h : h + 1, :] - cumt[:, h : h + 1]
        b = exct[:, h : h + 1] - exc[h : h + 1, :]
        e = jnp.exp(jnp.minimum(a, b))
        dec[h] = jnp.where(diag, 2.0, e).astype(BF)

    tok_in.wait()
    for c in range(16):
        tt = tok[:, 128 * c : 128 * c + 128].T
        for k in range(8):
            b = 8 * c + k
            tokt[b % 2, b // 2] = tt[16 * k : 16 * k + 16, :]
    tok_out = remote(tokt.at[1 - core], ts, sib_s.at[1], sib_r.at[1], sib)
    tok_out.start()

    for i in range(SUB):
        far_copy(i).wait_recv()
        for d in range(3):
            near_copy(d, i).start()
        pass_copy(0, i).start()
        for h in range(8 * i, 8 * i + 8):
            decays(h)

    def project(shard, first):
        k = pl.ds(pl.multiple_of(shard * 512, 512), 512)
        for c in range(3):
            cols = pl.ds(768 * c, 768)
            v = mm(tok[:, k], wf[k, cols], NN)
            if first:
                acc[:, cols] = v
            else:
                acc[:, cols] += v

    own_in.wait()
    project(f, True)
    for i in range(SUB):
        for d in range(3):
            remote(
                wf.at[piece(far_f, others[d], i)], wf.at[piece(far_f, others[d], i)],
                nb_s.at[d, i], nb_r.at[d, i], peers[ndims[d]],
            ).wait_recv()
            pass_copy(1 + d, i).start()
    go_in.wait()
    for c in range(16):
        gtr[128 * c : 128 * c + 128, :] = go[:, 128 * c : 128 * c + 128].T
    own_out.wait_recv()
    project(zh * 2 + 1 - core, False)
    project(far_f, False)
    for i in range(SUB):
        for j in range(4):
            p = piece(sibfar_f, colour if j == 0 else others[j - 1], i)
            remote(wf.at[p], wf.at[p], sf_s.at[j, i], sf_r.at[j, i], sib).wait_recv()
    project(sibfar_f, False)

    bmat[...] = acc[:, INNER : INNER + N].astype(BF)
    cmat[...] = acc[:, INNER + N : COLS].astype(BF)
    for c in range(18):
        xt[128 * c : 128 * c + 128, :] = acc[:, 128 * c : 128 * c + 128].astype(BF).T

    def head(h):
        return pl.ds(pl.multiple_of(h * PS, PS), PS)

    def sending(k, src, dst, p):
        return remote(src.at[p], dst.at[s], ssem.at[k, p], rsem.at[k, s], (p, f))

    def arriving(k, src, dst, p):
        return remote(src.at[p], dst.at[p], ssem.at[k, p], rsem.at[k, p], (p, f))

    def staged(k, src, dst, sign, wait, compute):
        def ship(t):
            @pl.when(t > 0)
            def _():
                sending(k, src, dst, peer(2 * t, sign)).start()

            sending(k, src, dst, peer(2 * t + 1, sign)).start()

        @pl.loop(0, 16)
        def _(t):
            if wait is not None:

                @pl.when(t > 0)
                def _():
                    arriving(*wait, peer(2 * t, sign)).wait_recv()

                arriving(*wait, peer(2 * t + 1, sign)).wait_recv()
            compute([peer(2 * t, sign), peer(2 * t + 1, sign)])
            if dst is not None:

                @pl.when(t > 0)
                def _():
                    ship(t - 1)

        if dst is not None:
            ship(15)

    def state(hs):
        for h in hs:
            xv = xt[head(h), :].astype(F32)
            r = rows[h]
            xs[h, pl.ds(0, PS), :] = (xv * r[2:3, :]).astype(BF)
            xs[h, pl.ds(PS, PS), :] = (xv * r[3:4, :]).astype(BF)
        for h in hs:
            up1[h] = mm(xs[h], bmat[...], NN).astype(BF)

    staged(0, up1, in1, 1, None, state)
    in1[s] = up1[s]

    aff[...] = mm(bmat[...], xt[pl.ds(INNER + N, N), :], NN).astype(BF)

    @pl.loop(0, H // 2)
    def _(t):
        for h in (2 * t, 2 * t + 1):
            y[h] = mm(xt[head(h), :], aff[...] * dec[h], NN)

    @pl.loop(1, 32)
    def _(o):
        p = peer(o)
        remote(tot.at[p], tin.at[p], tsem.at[p], trsem.at[p], (p, f)).wait_recv()
        arriving(0, up1, in1, p).wait_recv()

    def scan(src, dst, fwd, rev):
        def one(i, carry):
            a, b = carry
            k = 31 - i
            dst[i, pl.ds(fwd, PS), :] = a.astype(BF)
            dst[k, pl.ds(rev, PS), :] = b.astype(BF)
            a = jnp.exp(tin[i][0:1, :]) * a + src[i, pl.ds(fwd, PS), :].astype(F32)
            b = jnp.exp(tin[k][0:1, :]) * b + src[k, pl.ds(rev, PS), :].astype(F32)
            return a, b

        zero = jnp.zeros((PS, N), F32)
        lax.fori_loop(0, 32, one, (zero, zero))

    scan(in1, down1, 0, PS)

    @pl.loop(1, 32)
    def _(o):
        sending(1, down1, ent, peer(o)).start()

    ent[s] = down1[s]

    def mixture(hs):
        for h in hs:
            r = rows[h]
            car = mm(ent[h], xt[pl.ds(INNER + N, N), :], NN)
            mix = y[h] + r[0:1, :] * car[:PS] + r[1:2, :] * car[PS:]
            ms = jnp.sum(mix * mix, axis=0, keepdims=True) * (1.0 / PS)
            inv = 1.0 / jnp.sqrt(ms + EPS)
            z = mix * inv
            outt[head(h), :] = z.astype(BF)
            gv = gtr[head(h), :].astype(F32)
            m = jnp.sum(gv * z, axis=0, keepdims=True) * (1.0 / PS)
            gr = (gv - z * m) * inv
            gm[h] = gr.astype(BF)
            gmw[h, pl.ds(0, PS), :] = (gr * r[0:1, :]).astype(BF)
            gmw[h, pl.ds(PS, PS), :] = (gr * r[1:2, :]).astype(BF)
        for h in hs:
            up2[h] = mm(gmw[h], cmat[...], NN).astype(BF)

    staged(2, up2, in2, -1, (1, down1, ent), mixture)
    in2[s] = up2[s]

    gaff[...] = jnp.zeros_like(gaff)
    dct[...] = jnp.zeros_like(dct)
    dbt[...] = jnp.zeros_like(dbt)

    @pl.loop(0, H // 2)
    def _(t):
        total = None
        for h in (2 * t, 2 * t + 1):
            d = dec[h]
            gh = gm[h]
            y[h] = mm(gh, aff[...] * d, NT)
            gw = mm(xt[head(h), :], gh, TN) * d.astype(F32)
            total = gw if total is None else total + gw
        gaff[...] += total
        pair = pl.ds(2 * t, 2)
        dct[...] += mm(ent[pair].reshape(256, N), gmw[pair].reshape(256, T), TN)

    for c in range(16):
        outn[:, 128 * c : 128 * c + 128] = outt[128 * c : 128 * c + 128, :].T
    out_copy = pltpu.make_async_copy(outn, out_hbm, lsem.at[3])
    out_copy.start()

    tok_out.wait_recv()

    def block(r):
        p = here
        for d in range(6):
            if (r >> d) & 1:
                p = flip(d, *p)
        return p[2] * 32 + p[1] * 8 + p[0] * 2 + p[3]

    for r in range(64):
        b = block(r)
        ta[r] = tokt[core, b]
        tb[r] = ts[b]

    @pl.loop(1, 32)
    def _(o):
        arriving(2, up2, in2, peer(o)).wait_recv()

    scan(in2, down2, PS, 0)

    @pl.loop(1, 32)
    def _(o):
        sending(3, down2, adj, peer(o)).start()

    adj[s] = down2[s]
    ga = gaff[...].astype(BF)
    dct[...] += mm(xt[pl.ds(INNER, N), :], ga, NN)
    dbt[...] += mm(xt[pl.ds(INNER + N, N), :], ga, NT)
    g[:, INNER + N : COLS] = dct[...].astype(BF).T

    def finish(hs):
        total = None
        for h in hs:
            r = rows[h]
            car = mm(adj[h], xt[pl.ds(INNER, N), :], NN)
            gx = y[h] + r[2:3, :] * car[:PS] + r[3:4, :] * car[PS:]
            grad[head(h), :] = gx.astype(BF)
            v = mm(adj[h], xs[h], TN)
            total = v if total is None else total + v
        dbt[...] += total

    staged(3, None, None, -1, (3, down2, adj), finish)
    for c in range(16):
        g[:, 128 * c : 128 * c + 128] = grad[128 * c : 128 * c + 128, :].T
    g[:, INNER : INNER + N] = dbt[...].astype(BF).T

    g_out = remote(g, gs, sib_s.at[2], sib_r.at[2], sib)
    g_out.start()

    def tokens_part(i):
        r = pl.ds(512 * i, 512)
        tok[:, r] = mm(g[...], wf[r, :], NT).astype(BF)

    tokens_part(0)
    tokens_part(1)
    g_out.wait_recv()

    def product(c, half):
        ids = order(c)[32 * half : 32 * half + 32]
        la = jnp.concatenate([ta[r] for r in ids], axis=0)
        lb = jnp.concatenate([tb[r] for r in ids], axis=0)
        cols = pl.ds(c * CW, CW)
        return (mm(la, g[:, cols], NN) + mm(lb, gs[:, cols], NN)).reshape(32, 16, CW)

    def halve(c, k):
        p = pl.ds(OFF[k], 32 >> k)
        return remote(sb.at[c, p], rb.at[c, p], wsem.at[c, k], wrsem.at[c, k], peers[(c + k) % 6])

    for c in range(6):
        sb[c, pl.ds(0, 32)] = product(c, 1).astype(BF)
        halve(c, 0).start()
    for c in range(6):
        part[c] = product(c, 0)
    tokens_part(2)
    tokens_part(3)
    gt_copy = pltpu.make_async_copy(tok, gt_hbm, lsem.at[4])
    gt_copy.start()
    for k in range(1, 6):
        n = 64 >> k
        m = n // 2
        for c in range(6):
            halve(c, k - 1).wait_recv()
            hi = part[c, pl.ds(m, m)] + rb[c, pl.ds(OFF[k - 1] + m, m)].astype(F32)
            sb[c, pl.ds(OFF[k], m)] = hi.astype(BF)
            halve(c, k).start()
        for c in range(6):
            part[c, pl.ds(0, m)] += rb[c, pl.ds(OFF[k - 1], m)].astype(F32)
    for c in range(6):
        halve(c, 5).wait_recv()
        gw_ref[:, pl.ds(c * CW, CW)] = part[c, 0] + rb[c, OFF[5]].astype(F32)

    for i in range(SUB):
        far_copy(i).wait_send()
        for d in range(3):
            near_copy(d, i).wait_send()
        for j in range(4):
            pass_copy(j, i).wait_send()
    own_out.wait_send()
    tok_out.wait_send()
    g_out.wait_send()

    @pl.loop(1, 32)
    def _(o):
        p = peer(o)
        remote(tot.at[p], tin.at[s], tsem.at[p], trsem.at[s], (p, f)).wait_send()
        sending(0, up1, in1, p).wait_send()
        sending(1, down1, ent, p).wait_send()
        sending(2, up2, in2, p).wait_send()
        sending(3, down2, adj, p).wait_send()

    for c in range(6):
        for k in range(6):
            halve(c, k).wait_send()
    out_copy.wait()
    gt_copy.wait()


def on_device(tokens, w_in, log_decay, grad_out):
    v = pl.BlockSpec(memory_space=pltpu.VMEM)
    a = pl.BlockSpec(memory_space=pl.ANY)
    vm = pltpu.VMEM
    st = vm((H, 2 * PS, N), BF)
    dma = pltpu.SemaphoreType.DMA
    out, gt, gw = pl.pallas_call(
        kernel,
        name="mixer_step",
        out_shape=(
            jax.ShapeDtypeStruct((T, INNER), BF),
            jax.ShapeDtypeStruct((T, D), BF),
            jax.ShapeDtypeStruct((16, COLS), F32),
        ),
        in_specs=[a, a, v, a],
        out_specs=(a, a, v),
        scratch_shapes=[
            vm((D, COLS), BF),
            vm((T, D), BF),
            vm((2, 64, 16, T), BF),
            vm((64, 16, T), BF),
            vm((64, 16, T), BF),
            vm((64, 16, T), BF),
            vm((T, INNER), BF),
            vm((INNER, T), BF),
            vm((T, COLS), F32),
            vm((COLS, T), BF),
            vm((H, 8, T), F32),
            vm((H, 8, N), F32),
            vm((H, 8, N), F32),
            vm((H, T, T), BF),
            vm((T, T), BF),
            vm((H, PS, T), F32),
            vm((H, PS, T), BF),
            vm((H, 2 * PS, T), BF),
            vm((H, 2 * PS, T), BF),
            vm((T, T), F32),
            vm((N, T), F32),
            vm((N, T), F32),
            vm((T, N), BF),
            vm((T, N), BF),
            st, st, st, st, st, st, st, st,
            vm((INNER, T), BF),
            vm((T, INNER), BF),
            vm((INNER, T), BF),
            vm((T, COLS), BF),
            vm((T, COLS), BF),
            vm((6, 32, 16, CW), F32),
            vm((6, 63, 16, CW), BF),
            vm((6, 63, 16, CW), BF),
            dma((5,)),
            dma((SUB,)),
            dma((SUB,)),
            dma((3, SUB)),
            dma((3, SUB)),
            dma((4, SUB)),
            dma((4, SUB)),
            dma((3,)),
            dma((3,)),
            dma((4, 32)),
            dma((4, 32)),
            dma((32,)),
            dma((32,)),
            dma((6, 6)),
            dma((6, 6)),
        ],
        compiler_params=pltpu.CompilerParams(
            collective_id=0, has_side_effects=True, vmem_limit_bytes=60 * 1024 * 1024
        ),
    )(tokens[0], w_in, log_decay[0], grad_out[0])
    return out[None], gt[None], gw


def solution(mesh):
    return jax.shard_map(
        on_device,
        mesh=mesh,
        in_specs=(
            P("fsdp", "seq", None),
            P("fsdp", None),
            P("fsdp", None, "seq"),
            P("fsdp", "seq", None),
        ),
        out_specs=(P("fsdp", "seq", None), P("fsdp", "seq", None), P(("seq", "fsdp"), None)),
        check_vma=False,
    )
```

```python
import functools
import jax
import jax.numpy as jnp
from jax import lax
from jax.experimental import pallas as pl
from jax.experimental.pallas import tpu as pltpu
from jax.sharding import PartitionSpec as P

BF = jnp.bfloat16
F32 = jnp.float32
EPS = 1e-5
H, PS, N, T, D, INNER, COLS = 32, 64, 128, 256, 2048, 2048, 2304
MESH = pl.DeviceIdType.MESH
NN = (((1,), (0,)), ((), ()))
NT = (((1,), (1,)), ((), ()))
TN = (((0,), (0,)), ((), ()))
CW = COLS // 6
OFF = [0, 32, 48, 56, 60, 62]
PIECES = 9


def mm(a, b, dims):
    return lax.dot_general(a, b, dims, preferred_element_type=F32)


def place():
    s = lax.axis_index("seq")
    f = lax.axis_index("fsdp")
    return s % 4, (s // 4) % 4, s // 16, f // 2, f % 2


def device(x, y, zl, zh, core):
    return (zl * 16 + y * 4 + x, zh * 2 + core)


def flip(dim, x, y, zl, zh):
    if dim == 0:
        x = x + 1 - 2 * (x % 2)
    elif dim == 1:
        x = 3 - x
    elif dim == 2:
        y = y + 1 - 2 * (y % 2)
    elif dim == 3:
        y = 3 - y
    elif dim == 4:
        zl = 1 - zl
    else:
        zl, zh = 1 - zl, 1 - zh
    return x, y, zl, zh


def order(color):
    dims = [(color + k) % 6 for k in range(6)]
    found = []
    for i in range(64):
        r = 0
        for k in range(6):
            if (i >> (5 - k)) & 1:
                r |= 1 << dims[k]
        found.append(r)
    return found


def remote(src, dst, ssem, rsem, to):
    return pltpu.make_async_remote_copy(src, dst, ssem, rsem, to, MESH)


def kernel(
    tok_hbm, w_hbm, log_ref, go_hbm,
    out_hbm, gt_hbm, gw_ref,
    wf, tok, tokt, ts, ta, tb, go, gtr, xt, rows, tot, tin,
    dec, aff, y, gm, gmw, xs, gaff, dct, dbt, bmat, cmat,
    up1, in1, down1, ent, up2, in2, down2, adj,
    outt, outn, grad, g, gs, part, sb, rb,
    lsem, far_s, far_r, nb_s, nb_r, sf_s, sf_r, sib_s, sib_r, gsib_s, gsib_r,
    ssem, rsem, tsem, wsem, wrsem,
):
    s = lax.axis_index("seq")
    f = lax.axis_index("fsdp")
    x, y_, zl, zh, core = place()
    here = (x, y_, zl, zh)
    sib = device(*here, 1 - core)
    far = device(*flip(5, *here), core)
    peers = [device(*flip(d, *here), core) for d in range(6)]
    barrier = pltpu.get_barrier_semaphore()

    def peer(o, sign=1):
        px = lax.rem(x + 4 + sign * (o % 4), 4)
        py = lax.rem(y_ + 4 + sign * ((o // 4) % 4), 4)
        pz = lax.rem(zl + o // 16, 2)
        return pz * 16 + py * 4 + px

    @pl.loop(1, 32)
    def _(o):
        pl.semaphore_signal(barrier, inc=1, device_id=(peer(o), f), device_id_type=MESH)

    def across(dims):
        p = here
        for d in dims:
            p = flip(d, *p)
        return device(*p, core)

    further = [(3, 5), (4, 5), (3, 4, 5), (0, 5), (0, 4, 5), (1, 5), (0, 1, 5)]
    greeted = [sib, far] + [across(d) for d in further]
    for q in greeted:
        pl.semaphore_signal(barrier, inc=1, device_id=q, device_id_type=MESH)

    def whole(i):
        return pl.ds(pl.multiple_of(i * 512, 512), 512)

    tok_in = pltpu.make_async_copy(tok_hbm, tok, lsem.at[0])
    go_in = pltpu.make_async_copy(go_hbm, go, lsem.at[1])
    own_in = pltpu.make_async_copy(w_hbm, wf.at[whole(f)], lsem.at[2])
    tok_in.start()
    own_in.start()
    go_in.start()

    ri = lax.broadcasted_iota(jnp.int32, (T, T), 0)
    ci = lax.broadcasted_iota(jnp.int32, (T, T), 1)
    log = log_ref[...]
    cum = lax.dot_general(
        log, (ri <= ci).astype(F32), NN, precision=lax.Precision.HIGHEST, preferred_element_type=F32
    )
    exc = cum - log
    last = cum[:, T - 1 : T]
    cumt = cum.T
    exct = exc.T
    fac = (jnp.exp(cum), jnp.exp(last - exc), jnp.exp(last - cum), jnp.exp(exc))
    lastb = jnp.broadcast_to(last, (H, N))
    for h in range(H):
        for k in range(4):
            rows[h, k : k + 1, :] = fac[k][h : h + 1, :]
    for h in range(8):
        four = [lastb[8 * k + h : 8 * k + h + 1, :] for k in range(4)]
        v = jnp.concatenate(four + four, axis=0)
        for k in range(4):
            tot[4 * h + k] = v

    pl.semaphore_wait(barrier, 31 + len(greeted))

    far_f = (1 - zh) * 2 + core
    sibfar_f = (1 - zh) * 2 + 1 - core
    q0, q1 = (x + zl) % 2, (y_ + zl) % 2
    colour = q0 + 2 * q1
    others = [(1 - q0) + 2 * q1, q0 + 2 * (1 - q1), (1 - q0) + 2 * (1 - q1)]
    ndims = [0, 2, 4]

    def piece(shard, quarter, i):
        r = pl.ds(pl.multiple_of(shard * 512 + quarter * 128, 128), 128)
        return r, pl.ds(256 * ((i + 8) % 9), 256)

    def far_copy(i):
        mine = pl.ds(pl.multiple_of(others[2] * 128, 128), 128)
        p = piece(f, others[2], i)
        return remote(w_hbm.at[mine, p[1]], wf.at[p], far_s.at[i], far_r.at[i], far)

    def near_copy(d, i):
        p = piece(far_f, colour, i)
        return remote(wf.at[p], wf.at[p], nb_s.at[d, i], nb_r.at[d, i], peers[ndims[d]])

    def pass_copy(j, i):
        p = piece(far_f, colour if j == 0 else others[j - 1], i)
        return remote(wf.at[p], wf.at[p], sf_s.at[j, i], sf_r.at[j, i], sib)

    own_out = remote(w_hbm, wf.at[whole(f)], sib_s.at[0], sib_r.at[0], sib)
    for i in range(PIECES):
        far_copy(i).start()
    own_out.start()

    def tot_copy(o):
        p = peer(o)
        return remote(tot.at[p], tin.at[s], tsem.at[0], tsem.at[1], (p, f))

    @pl.loop(1, 32)
    def _(o):
        tot_copy(o).start()

    tin[s] = tot[s]
    most = pl.ds(0, 31)

    diag = ri == ci

    def decays(h):
        a = cum[h : h + 1, :] - cumt[:, h : h + 1]
        b = exct[:, h : h + 1] - exc[h : h + 1, :]
        e = jnp.exp(jnp.minimum(a, b))
        dec[h] = jnp.where(diag, 2.0, e).astype(BF)

    tok_in.wait()
    for c in range(16):
        tt = tok[:, 128 * c : 128 * c + 128].T
        for k in range(8):
            b = 8 * c + k
            tokt[b % 2, b // 2] = tt[16 * k : 16 * k + 16, :]
    tok_out = remote(tokt.at[1 - core], ts, sib_s.at[1], sib_r.at[1], sib)
    tok_out.start()

    go_in.wait()
    for c in range(16):
        gtr[128 * c : 128 * c + 128, :] = go[:, 128 * c : 128 * c + 128].T

    def head(h):
        return pl.ds(pl.multiple_of(h * PS, PS), PS)

    def transfer(k, q, p):
        src, dst = ((up1, in1), (down1, ent), (up2, in2), (down2, adj))[k]
        a = src.at[q, p] if k % 2 else src.at[q, :, p]
        b = dst.at[q, :, s] if k % 2 else dst.at[q, s]
        return remote(a, b, ssem.at[k, q], rsem.at[k, q], (p, f))

    def send(k, q):
        src, dst = ((up1, in1), (down1, ent), (up2, in2), (down2, adj))[k]

        @pl.loop(1, 32)
        def _(o):
            transfer(k, q, peer(o)).start()

        if k % 2:
            dst[q, :, s] = src[q, s]
        else:
            dst[q, s] = src[q, :, s]

    def whole_chunk(k, q):
        src, dst = ((up1, in1), (down1, ent), (up2, in2), (down2, adj))[k]
        a = src.at[q, most] if k % 2 else src.at[q, :, most]
        b = dst.at[q, :, most] if k % 2 else dst.at[q, most]
        return a, b

    def arrived(k, q):
        _, b = whole_chunk(k, q)
        remote(b, b, ssem.at[k, q], rsem.at[k, q], sib).wait_recv()

    def left(k, q):
        a, _ = whole_chunk(k, q)
        remote(a, a, ssem.at[k, q], rsem.at[k, q], sib).wait_send()

    def pairs(q, body):
        @pl.loop(0, 4)
        def _(t):
            body([(8 * q + 2 * t + i, 2 * t + i) for i in range(2)])

    def quarter(ref, q, i):
        return jnp.concatenate(
            [ref[q, k, pl.ds(4 * i, 4)].reshape(PS, N) for k in range(2)], axis=0
        )

    def store(ref, q, i, v):
        v = v.reshape(2, 4, 16, N)
        for k in range(2):
            ref[q, k, pl.ds(4 * i, 4)] = v[k]

    ctall = pl.ds(INNER + N, N)
    btall = pl.ds(INNER, N)

    def project(q):
        cols = pl.ds(512 * q, 512)
        v = mm(tok[...], wf[:, cols], NN).astype(BF)
        for c in range(4):
            xt[512 * q + 128 * c : 512 * q + 128 * c + 128, :] = v[:, 128 * c : 128 * c + 128].T

    def project_last():
        v = mm(tok[...], wf[:, INNER:COLS], NN).astype(BF)
        bmat[...] = v[:, :N]
        cmat[...] = v[:, N:]
        xt[btall, :] = v[:, :N].T
        xt[ctall, :] = v[:, N:].T
        aff[...] = mm(v[:, :N], xt[ctall, :], NN).astype(BF)

    def states(q):
        def body(hs):
            for h, i in hs:
                xv = xt[head(h), :].astype(F32)
                r = rows[h]
                xs[h, pl.ds(0, PS), :] = (xv * r[2:3, :]).astype(BF)
                xs[h, pl.ds(PS, PS), :] = (xv * r[3:4, :]).astype(BF)
            for h, i in hs:
                store(up1, q, i, mm(xs[h], bmat[...], NN).astype(BF))

        pairs(q, body)
        send(0, q)

    def local_forward(q):
        def body(hs):
            for h, _ in hs:
                y[h] = mm(xt[head(h), :], aff[...] * dec[h], NN)

        pairs(q, body)

    def scan(k, q, fwd, rev):
        src, dst = ((in1, down1), None, (in2, down2))[k]
        arrived(k, q)

        def one(i, carry):
            a, b = carry
            j = 31 - i
            dst[q, i, fwd] = a.astype(BF)
            dst[q, j, rev] = b.astype(BF)
            a = tin[i, q : q + 1, :] * a + src[q, i, fwd].astype(F32)
            b = tin[j, q : q + 1, :] * b + src[q, j, rev].astype(F32)
            return a, b

        zero = jnp.zeros((16, N), F32)
        lax.fori_loop(0, 32, one, (zero, zero), unroll=4)
        send(k + 1, q)

    def mixture(q):
        arrived(1, q)

        def body(hs):
            for h, i in hs:
                r = rows[h]
                car = mm(quarter(ent, q, i), xt[ctall, :], NN)
                mix = y[h] + r[0:1, :] * car[:PS] + r[1:2, :] * car[PS:]
                ms = jnp.sum(mix * mix, axis=0, keepdims=True) * (1.0 / PS)
                inv = 1.0 / jnp.sqrt(ms + EPS)
                z = mix * inv
                outt[head(h), :] = z.astype(BF)
                gv = gtr[head(h), :].astype(F32)
                m = jnp.sum(gv * z, axis=0, keepdims=True) * (1.0 / PS)
                gr = (gv - z * m) * inv
                gm[h] = gr.astype(BF)
                gmw[h, pl.ds(0, PS), :] = (gr * r[0:1, :]).astype(BF)
                gmw[h, pl.ds(PS, PS), :] = (gr * r[1:2, :]).astype(BF)
            for h, i in hs:
                store(up2, q, i, mm(gmw[h], cmat[...], NN).astype(BF))

        pairs(q, body)
        send(2, q)

    def local_backward(q):
        def body(hs):
            total = None
            for h, i in hs:
                d = dec[h]
                gh = gm[h]
                y[h] = mm(gh, aff[...] * d, NT)
                gw = mm(xt[head(h), :], gh, TN) * d.astype(F32)
                total = gw if total is None else total + gw
            gaff[...] += total
            e = jnp.concatenate([quarter(ent, q, i) for _, i in hs], axis=0)
            w = jnp.concatenate([gmw[h] for h, _ in hs], axis=0)
            dct[...] += mm(e, w, TN)

        pairs(q, body)

    def finish(q):
        arrived(3, q)

        def body(hs):
            total = None
            for h, i in hs:
                r = rows[h]
                e = quarter(adj, q, i)
                car = mm(e, xt[btall, :], NN)
                gx = y[h] + r[2:3, :] * car[:PS] + r[3:4, :] * car[PS:]
                grad[head(h), :] = gx.astype(BF)
                v = mm(e, xs[h], TN)
                total = v if total is None else total + v
            dbt[...] += total

        pairs(q, body)
        for c in range(4 * q, 4 * q + 4):
            g[:, 128 * c : 128 * c + 128] = grad[128 * c : 128 * c + 128, :].T
        g_copy(q).start()

    def g_copy(q):
        cols = pl.ds(512 * q, 512 if q < 4 else 256)
        return remote(g.at[:, cols], gs.at[:, cols], gsib_s.at[q], gsib_r.at[q], sib)

    todo = list(range(H))

    def some(n):
        for h in todo[:n]:
            decays(h)
        del todo[:n]

    gaff[...] = jnp.zeros_like(gaff)
    dct[...] = jnp.zeros_like(dct)
    dbt[...] = jnp.zeros_like(dbt)
    some(6)
    for i in range(PIECES + 2):
        if i < PIECES:
            far_copy(i).wait_recv()
            for d in range(3):
                near_copy(d, i).start()
            pass_copy(0, i).start()
        if 1 <= i <= PIECES:
            for d in range(3):
                p = piece(far_f, others[d], i - 1)
                remote(
                    wf.at[p], wf.at[p], nb_s.at[d, i - 1], nb_r.at[d, i - 1], peers[ndims[d]]
                ).wait_recv()
                pass_copy(1 + d, i - 1).start()
        if i >= 2:
            for j in range(4):
                p = piece(sibfar_f, colour if j == 0 else others[j - 1], i - 2)
                remote(wf.at[p], wf.at[p], sf_s.at[j, i - 2], sf_r.at[j, i - 2], sib).wait_recv()
            if i == 2:
                own_in.wait()
                own_out.wait_recv()
                project_last()
            elif i % 2 == 0:
                project(i // 2 - 2)
                states(i // 2 - 2)
        if i not in (2, 4, 6, 8, 10):
            some(6)
    some(H)
    local_forward(0)
    local_forward(1)
    remote(
        tin.at[most], tin.at[most], tsem.at[0], tsem.at[1], sib
    ).wait_recv()
    tin[...] = jnp.exp(tin[...])

    def block(r):
        p = here
        for d in range(6):
            if (r >> d) & 1:
                p = flip(d, *p)
        return p[2] * 32 + p[1] * 8 + p[0] * 2 + p[3]

    def relay_tokens():
        tok_out.wait_recv()
        for r in range(64):
            b = block(r)
            ta[r] = tokt[core, b]
            tb[r] = ts[b]

    out_copy = pltpu.make_async_copy(outn, out_hbm, lsem.at[3])

    def give_output():
        for c in range(16):
            outn[:, 128 * c : 128 * c + 128] = outt[128 * c : 128 * c + 128, :].T
        out_copy.start()

    def close_affinity():
        ga = gaff[...].astype(BF)
        dct[...] += mm(xt[btall, :], ga, NN)
        dbt[...] += mm(xt[ctall, :], ga, NT)
        g[:, INNER + N : COLS] = dct[...].astype(BF).T

    def product(c, half):
        ids = order(c)[32 * half : 32 * half + 32]
        la = jnp.concatenate([ta[r] for r in ids], axis=0)
        lb = jnp.concatenate([tb[r] for r in ids], axis=0)
        cols = pl.ds(c * CW, CW)
        v = mm(la, g[:, cols], NN) + mm(lb, gs[:, cols], NN)
        return v.reshape(32, 16, CW).astype(BF)

    def halve(c, k):
        p = pl.ds(OFF[k], 32 >> k)
        return remote(sb.at[c, p], rb.at[c, p], wsem.at[c, k], wrsem.at[c, k], peers[(c + k) % 6])

    def direct(c, i):
        dims = [(c + 3 + b) % 6 for b in range(3) if (i >> (2 - b)) & 1]
        return remote(
            part.at[c, i], rb.at[c, OFF[3] + i - 1], wsem.at[c, 3], wrsem.at[c, 3], across(dims)
        )

    def first(c):
        sb[c, pl.ds(0, 32)] = product(c, 1)
        halve(c, 0).start()

    def tokens_part(i):
        r = pl.ds(512 * i, 512)
        tok[:, r] = mm(g[...], wf[r, :], NT).astype(BF)

    scan(0, 0, 0, 1)
    scan(0, 1, 0, 1)
    local_forward(2)
    scan(0, 2, 0, 1)
    mixture(0)
    local_forward(3)
    scan(0, 3, 0, 1)
    mixture(1)
    local_backward(0)
    mixture(2)
    scan(2, 0, 1, 0)
    local_backward(1)
    mixture(3)
    scan(2, 1, 1, 0)
    local_backward(2)
    give_output()
    scan(2, 2, 1, 0)
    local_backward(3)
    relay_tokens()
    finish(0)
    scan(2, 3, 1, 0)
    close_affinity()
    finish(1)
    g_copy(0).wait_recv()
    first(0)
    finish(2)
    g_copy(1).wait_recv()
    first(1)
    finish(3)
    g[:, INNER : INNER + N] = dbt[...].astype(BF).T
    g_copy(4).start()
    g_copy(2).wait_recv()
    first(2)
    first(3)
    g_copy(3).wait_recv()
    first(4)
    g_copy(4).wait_recv()
    first(5)
    for c in range(6):
        part[c] = product(c, 0)
    tokens_part(0)
    tokens_part(1)
    tokens_part(2)
    tokens_part(3)
    gt_copy = pltpu.make_async_copy(tok, gt_hbm, lsem.at[4])
    gt_copy.start()
    for k in range(1, 4):
        n = 64 >> k
        m = n // 2
        for c in range(6):
            halve(c, k - 1).wait_recv()
            if k < 3:
                sb[c, pl.ds(OFF[k], m)] = part[c, pl.ds(m, m)] + rb[c, pl.ds(OFF[k - 1] + m, m)]
                halve(c, k).start()
            else:
                part[c, pl.ds(0, n)] += rb[c, pl.ds(OFF[k - 1], n)]
                for i in range(7, 0, -1):
                    direct(c, i).start()
        if k < 3:
            for c in range(6):
                part[c, pl.ds(0, m)] += rb[c, pl.ds(OFF[k - 1], m)]
    rest = pl.ds(OFF[3], 7)
    for c in range(6):
        remote(rb.at[c, rest], rb.at[c, rest], wsem.at[c, 3], wrsem.at[c, 3], sib).wait_recv()
        v = part[c, 0].astype(F32)
        for i in range(7):
            v = v + rb[c, OFF[3] + i].astype(F32)
        gw_ref[:, pl.ds(c * CW, CW)] = v

    for i in range(PIECES):
        far_copy(i).wait_send()
        for d in range(3):
            near_copy(d, i).wait_send()
        for j in range(4):
            pass_copy(j, i).wait_send()
    own_out.wait_send()
    tok_out.wait_send()
    remote(tot.at[most], tot.at[most], tsem.at[0], tsem.at[1], sib).wait_send()
    for q in range(4):
        for k in range(4):
            left(k, q)
    for q in range(5):
        g_copy(q).wait_send()
    for c in range(6):
        for k in range(3):
            halve(c, k).wait_send()
        sent = pl.ds(1, 7)
        remote(
            part.at[c, sent], part.at[c, sent], wsem.at[c, 3], wrsem.at[c, 3], sib
        ).wait_send()
    out_copy.wait()
    gt_copy.wait()


def on_device(tokens, w_in, log_decay, grad_out):
    v = pl.BlockSpec(memory_space=pltpu.VMEM)
    a = pl.BlockSpec(memory_space=pl.ANY)
    vm = pltpu.VMEM
    st = vm((4, 2, 32, 16, N), BF)
    sr = vm((4, 32, 2, 16, N), BF)
    dma = pltpu.SemaphoreType.DMA
    out, gt, gw = pl.pallas_call(
        kernel,
        name="mixer_step",
        out_shape=(
            jax.ShapeDtypeStruct((T, INNER), BF),
            jax.ShapeDtypeStruct((T, D), BF),
            jax.ShapeDtypeStruct((16, COLS), F32),
        ),
        in_specs=[a, a, v, a],
        out_specs=(a, a, v),
        scratch_shapes=[
            vm((D, COLS), BF),
            vm((T, D), BF),
            vm((2, 64, 16, T), BF),
            vm((64, 16, T), BF),
            vm((64, 16, T), BF),
            vm((64, 16, T), BF),
            vm((T, INNER), BF),
            vm((INNER, T), BF),
            vm((COLS, T), BF),
            vm((H, 8, T), F32),
            vm((H, 8, N), F32),
            vm((H, 8, N), F32),
            vm((H, T, T), BF),
            vm((T, T), BF),
            vm((H, PS, T), F32),
            vm((H, PS, T), BF),
            vm((H, 2 * PS, T), BF),
            vm((H, 2 * PS, T), BF),
            vm((T, T), F32),
            vm((N, T), F32),
            vm((N, T), F32),
            vm((T, N), BF),
            vm((T, N), BF),
            st, sr, sr, st, st, sr, sr, st,
            vm((INNER, T), BF),
            vm((T, INNER), BF),
            vm((INNER, T), BF),
            vm((T, COLS), BF),
            vm((T, COLS), BF),
            vm((6, 32, 16, CW), BF),
            vm((6, 63, 16, CW), BF),
            vm((6, 63, 16, CW), BF),
            dma((5,)),
            dma((PIECES,)),
            dma((PIECES,)),
            dma((3, PIECES)),
            dma((3, PIECES)),
            dma((4, PIECES)),
            dma((4, PIECES)),
            dma((2,)),
            dma((2,)),
            dma((5,)),
            dma((5,)),
            dma((4, 4)),
            dma((4, 4)),
            dma((2,)),
            dma((6, 4)),
            dma((6, 4)),
        ],
        compiler_params=pltpu.CompilerParams(
            collective_id=0, has_side_effects=True, vmem_limit_bytes=60 * 1024 * 1024
        ),
    )(tokens[0], w_in, log_decay[0], grad_out[0])
    return out[None], gt[None], gw


def solution(mesh):
    return jax.shard_map(
        on_device,
        mesh=mesh,
        in_specs=(
            P("fsdp", "seq", None),
            P("fsdp", None),
            P("fsdp", None, "seq"),
            P("fsdp", "seq", None),
        ),
        out_specs=(P("fsdp", "seq", None), P("fsdp", "seq", None), P(("seq", "fsdp"), None)),
        check_vma=False,
    )
```

```python
import functools
import jax
import jax.numpy as jnp
from jax import lax
from jax.experimental import pallas as pl
from jax.experimental.pallas import tpu as pltpu
from jax.sharding import PartitionSpec as P

BF = jnp.bfloat16
F32 = jnp.float32
EPS = 1e-5
H, PS, N, T, D, INNER, COLS = 32, 64, 128, 256, 2048, 2048, 2304
MESH = pl.DeviceIdType.MESH
NN = (((1,), (0,)), ((), ()))
NT = (((1,), (1,)), ((), ()))
TN = (((0,), (0,)), ((), ()))
CW = COLS // 6
OFF = [0, 32, 48, 56, 60, 62]
PIECES = 9
GROUP = 4


def mm(a, b, dims):
    return lax.dot_general(a, b, dims, preferred_element_type=F32)


def place():
    s = lax.axis_index("seq")
    f = lax.axis_index("fsdp")
    return s % 4, (s // 4) % 4, s // 16, f // 2, f % 2


def device(x, y, zl, zh, core):
    return (zl * 16 + y * 4 + x, zh * 2 + core)


def flip(dim, x, y, zl, zh):
    if dim == 0:
        x = x + 1 - 2 * (x % 2)
    elif dim == 1:
        x = 3 - x
    elif dim == 2:
        y = y + 1 - 2 * (y % 2)
    elif dim == 3:
        y = 3 - y
    elif dim == 4:
        zl = 1 - zl
    else:
        zl, zh = 1 - zl, 1 - zh
    return x, y, zl, zh


def order(color):
    dims = [(color + k) % 6 for k in range(6)]
    found = []
    for i in range(64):
        r = 0
        for k in range(6):
            if (i >> (5 - k)) & 1:
                r |= 1 << dims[k]
        found.append(r)
    return found


def remote(src, dst, ssem, rsem, to):
    return pltpu.make_async_remote_copy(src, dst, ssem, rsem, to, MESH)


def kernel(
    tok_hbm, w_hbm, log_ref, go_hbm,
    out_hbm, gt_hbm, gw_ref,
    wf, tok, tokt, ts, ta, tb, go, gtr, xt, rows, tot, tin,
    dec, aff, y, gm, gmw, xs, gaff, dct, dbt, bmat, cmat,
    up1, in1, down1, ent, up2, in2, down2, adj,
    outt, outn, grad, g, gs, part, sb, rb,
    lsem, far_s, far_r, nb_s, nb_r, sf_s, sf_r, sib_s, sib_r, gsib_s, gsib_r,
    ssem, rsem, tsem, wsem, wrsem,
):
    s = lax.axis_index("seq")
    f = lax.axis_index("fsdp")
    x, y_, zl, zh, core = place()
    here = (x, y_, zl, zh)
    sib = device(*here, 1 - core)
    far = device(*flip(5, *here), core)
    peers = [device(*flip(d, *here), core) for d in range(6)]
    barrier = pltpu.get_barrier_semaphore()

    def peer(o, sign=1):
        px = lax.rem(x + 4 + sign * (o % 4), 4)
        py = lax.rem(y_ + 4 + sign * ((o // 4) % 4), 4)
        pz = lax.rem(zl + o // 16, 2)
        return pz * 16 + py * 4 + px

    @pl.loop(1, 32)
    def _(o):
        pl.semaphore_signal(barrier, inc=1, device_id=(peer(o), f), device_id_type=MESH)

    def across(dims):
        p = here
        for d in dims:
            p = flip(d, *p)
        return device(*p, core)

    further = [(3, 5), (4, 5), (3, 4, 5), (0, 5), (0, 4, 5), (1, 5), (0, 1, 5)]
    greeted = [sib, far] + [across(d) for d in further]
    for q in greeted:
        pl.semaphore_signal(barrier, inc=1, device_id=q, device_id_type=MESH)

    def whole(i):
        return pl.ds(pl.multiple_of(i * 512, 512), 512)

    tok_in = pltpu.make_async_copy(tok_hbm, tok, lsem.at[0])
    go_in = pltpu.make_async_copy(go_hbm, go, lsem.at[1])
    own_in = pltpu.make_async_copy(w_hbm, wf.at[whole(f)], lsem.at[2])
    tok_in.start()
    own_in.start()
    go_in.start()

    ri = lax.broadcasted_iota(jnp.int32, (T, T), 0)
    ci = lax.broadcasted_iota(jnp.int32, (T, T), 1)
    log = log_ref[...]
    cum = lax.dot_general(
        log, (ri <= ci).astype(F32), NN, precision=lax.Precision.HIGHEST, preferred_element_type=F32
    )
    exc = cum - log
    last = cum[:, T - 1 : T]
    cumt = cum.T
    exct = exc.T
    fac = (jnp.exp(cum), jnp.exp(last - exc), jnp.exp(last - cum), jnp.exp(exc))
    lastb = jnp.broadcast_to(last, (H, N))
    for h in range(H):
        for k in range(4):
            rows[h, k : k + 1, :] = fac[k][h : h + 1, :]
    for h in range(8):
        four = [lastb[8 * k + h : 8 * k + h + 1, :] for k in range(4)]
        v = jnp.concatenate(four + four, axis=0)
        for k in range(4):
            tot[4 * h + k] = v

    pl.semaphore_wait(barrier, 31 + len(greeted))

    far_f = (1 - zh) * 2 + core
    sibfar_f = (1 - zh) * 2 + 1 - core
    q0, q1 = (x + zl) % 2, (y_ + zl) % 2
    colour = q0 + 2 * q1
    others = [(1 - q0) + 2 * q1, q0 + 2 * (1 - q1), (1 - q0) + 2 * (1 - q1)]
    ndims = [0, 2, 4]

    def piece(shard, quarter, i):
        r = pl.ds(pl.multiple_of(shard * 512 + quarter * 128, 128), 128)
        return r, pl.ds(256 * ((i + 8) % 9), 256)

    def far_copy(i):
        mine = pl.ds(pl.multiple_of(others[2] * 128, 128), 128)
        p = piece(f, others[2], i)
        return remote(w_hbm.at[mine, p[1]], wf.at[p], far_s.at[i], far_r.at[i], far)

    def near_copy(d, i):
        p = piece(far_f, colour, i)
        return remote(wf.at[p], wf.at[p], nb_s.at[d, i], nb_r.at[d, i], peers[ndims[d]])

    def pass_copy(j, i):
        p = piece(far_f, colour if j == 0 else others[j - 1], i)
        return remote(wf.at[p], wf.at[p], sf_s.at[j, i], sf_r.at[j, i], sib)

    own_out = remote(w_hbm, wf.at[whole(f)], sib_s.at[0], sib_r.at[0], sib)
    for i in range(PIECES):
        far_copy(i).start()
    own_out.start()

    def tot_copy(o):
        p = peer(o)
        return remote(tot.at[p], tin.at[s], tsem.at[0], tsem.at[1], (p, f))

    @pl.loop(1, 32)
    def _(o):
        tot_copy(o).start()

    tin[s] = tot[s]
    most = pl.ds(0, 31)

    diag = ri == ci

    def decays(h):
        a = cum[h : h + 1, :] - cumt[:, h : h + 1]
        b = exct[:, h : h + 1] - exc[h : h + 1, :]
        e = jnp.exp(jnp.minimum(a, b))
        dec[h] = jnp.where(diag, 2.0, e).astype(BF)

    tok_in.wait()
    for c in range(16):
        tt = tok[:, 128 * c : 128 * c + 128].T
        for k in range(8):
            b = 8 * c + k
            tokt[b % 2, b // 2] = tt[16 * k : 16 * k + 16, :]
    tok_out = remote(tokt.at[1 - core], ts, sib_s.at[1], sib_r.at[1], sib)
    tok_out.start()

    go_in.wait()
    for c in range(16):
        gtr[128 * c : 128 * c + 128, :] = go[:, 128 * c : 128 * c + 128].T

    def head(h):
        return pl.ds(pl.multiple_of(h * PS, PS), PS)

    def transfer(k, q, p):
        src, dst = ((up1, in1), (down1, ent), (up2, in2), (down2, adj))[k]
        a = src.at[q, p] if k % 2 else src.at[q, :, p]
        b = dst.at[q, :, s] if k % 2 else dst.at[q, s]
        return remote(a, b, ssem.at[k, q], rsem.at[k, q], (p, f))

    def send(k, q):
        src, dst = ((up1, in1), (down1, ent), (up2, in2), (down2, adj))[k]

        @pl.loop(1, 32)
        def _(o):
            transfer(k, q, peer(o)).start()

        if k % 2:
            dst[q, :, s] = src[q, s]
        else:
            dst[q, s] = src[q, :, s]

    def whole_chunk(k, q):
        src, dst = ((up1, in1), (down1, ent), (up2, in2), (down2, adj))[k]
        a = src.at[q, most] if k % 2 else src.at[q, :, most]
        b = dst.at[q, :, most] if k % 2 else dst.at[q, most]
        return a, b

    def arrived(k, q):
        _, b = whole_chunk(k, q)
        remote(b, b, ssem.at[k, q], rsem.at[k, q], sib).wait_recv()

    def left(k, q):
        a, _ = whole_chunk(k, q)
        remote(a, a, ssem.at[k, q], rsem.at[k, q], sib).wait_send()

    def pairs(q, body):
        @pl.loop(0, 8 // GROUP)
        def _(t):
            body([(8 * q + GROUP * t + i, GROUP * t + i) for i in range(GROUP)])

    def quarter(ref, q, i):
        return jnp.concatenate(
            [ref[q, k, pl.ds(4 * i, 4)].reshape(PS, N) for k in range(2)], axis=0
        )

    def store(ref, q, i, v):
        v = v.reshape(2, 4, 16, N)
        for k in range(2):
            ref[q, k, pl.ds(4 * i, 4)] = v[k]

    ctall = pl.ds(INNER + N, N)
    btall = pl.ds(INNER, N)

    def project(q):
        cols = pl.ds(512 * q, 512)
        v = mm(tok[...], wf[:, cols], NN).astype(BF)
        for c in range(4):
            xt[512 * q + 128 * c : 512 * q + 128 * c + 128, :] = v[:, 128 * c : 128 * c + 128].T

    def project_last():
        v = mm(tok[...], wf[:, INNER:COLS], NN).astype(BF)
        bmat[...] = v[:, :N]
        cmat[...] = v[:, N:]
        xt[btall, :] = v[:, :N].T
        xt[ctall, :] = v[:, N:].T
        aff[...] = mm(v[:, :N], xt[ctall, :], NN).astype(BF)

    def states(q):
        def body(hs):
            for h, i in hs:
                xv = xt[head(h), :].astype(F32)
                r = rows[h]
                xs[h, pl.ds(0, PS), :] = (xv * r[2:3, :]).astype(BF)
                xs[h, pl.ds(PS, PS), :] = (xv * r[3:4, :]).astype(BF)
            for h, i in hs:
                store(up1, q, i, mm(xs[h], bmat[...], NN).astype(BF))

        pairs(q, body)
        send(0, q)

    def local_forward(q):
        def body(hs):
            for h, _ in hs:
                y[h] = mm(xt[head(h), :], aff[...] * dec[h], NN)

        pairs(q, body)

    def scan(k, q, fwd, rev):
        src, dst = ((in1, down1), None, (in2, down2))[k]
        arrived(k, q)

        def one(i, carry):
            a, b = carry
            j = 31 - i
            dst[q, i, fwd] = a.astype(BF)
            dst[q, j, rev] = b.astype(BF)
            a = tin[i, q : q + 1, :] * a + src[q, i, fwd].astype(F32)
            b = tin[j, q : q + 1, :] * b + src[q, j, rev].astype(F32)
            return a, b

        zero = jnp.zeros((16, N), F32)
        lax.fori_loop(0, 32, one, (zero, zero), unroll=32)
        send(k + 1, q)

    def mixture(q):
        arrived(1, q)

        def body(hs):
            for h, i in hs:
                r = rows[h]
                car = mm(quarter(ent, q, i), xt[ctall, :], NN)
                mix = y[h] + r[0:1, :] * car[:PS] + r[1:2, :] * car[PS:]
                ms = jnp.sum(mix * mix, axis=0, keepdims=True) * (1.0 / PS)
                inv = 1.0 / jnp.sqrt(ms + EPS)
                z = mix * inv
                outt[head(h), :] = z.astype(BF)
                gv = gtr[head(h), :].astype(F32)
                m = jnp.sum(gv * z, axis=0, keepdims=True) * (1.0 / PS)
                gr = (gv - z * m) * inv
                gm[h] = gr.astype(BF)
                gmw[h, pl.ds(0, PS), :] = (gr * r[0:1, :]).astype(BF)
                gmw[h, pl.ds(PS, PS), :] = (gr * r[1:2, :]).astype(BF)
            for h, i in hs:
                store(up2, q, i, mm(gmw[h], cmat[...], NN).astype(BF))

        pairs(q, body)
        send(2, q)

    def local_backward(q):
        def body(hs):
            total = None
            for h, i in hs:
                d = dec[h]
                gh = gm[h]
                y[h] = mm(gh, aff[...] * d, NT)
                gw = mm(xt[head(h), :], gh, TN) * d.astype(F32)
                total = gw if total is None else total + gw
            gaff[...] += total
            e = jnp.concatenate([quarter(ent, q, i) for _, i in hs], axis=0)
            w = jnp.concatenate([gmw[h] for h, _ in hs], axis=0)
            dct[...] += mm(e, w, TN)

        pairs(q, body)

    def finish(q):
        arrived(3, q)

        def body(hs):
            total = None
            for h, i in hs:
                r = rows[h]
                e = quarter(adj, q, i)
                car = mm(e, xt[btall, :], NN)
                gx = y[h] + r[2:3, :] * car[:PS] + r[3:4, :] * car[PS:]
                grad[head(h), :] = gx.astype(BF)
                v = mm(e, xs[h], TN)
                total = v if total is None else total + v
            dbt[...] += total

        pairs(q, body)
        for c in range(4 * q, 4 * q + 4):
            g[:, 128 * c : 128 * c + 128] = grad[128 * c : 128 * c + 128, :].T
        g_copy(q).start()

    def g_copy(q):
        cols = pl.ds(512 * q, 512 if q < 4 else 256)
        return remote(g.at[:, cols], gs.at[:, cols], gsib_s.at[q], gsib_r.at[q], sib)

    todo = list(range(H))

    def some(n):
        for h in todo[:n]:
            decays(h)
        del todo[:n]

    gaff[...] = jnp.zeros_like(gaff)
    dct[...] = jnp.zeros_like(dct)
    dbt[...] = jnp.zeros_like(dbt)
    def from_far(i):
        far_copy(i).wait_recv()
        for d in range(3):
            near_copy(d, i).start()
        pass_copy(0, i).start()

    def from_near(i):
        for d in range(3):
            p = piece(far_f, others[d], i)
            remote(
                wf.at[p], wf.at[p], nb_s.at[d, i], nb_r.at[d, i], peers[ndims[d]]
            ).wait_recv()
            pass_copy(1 + d, i).start()

    def from_sibling(i):
        for j in range(4):
            p = piece(sibfar_f, colour if j == 0 else others[j - 1], i)
            remote(wf.at[p], wf.at[p], sf_s.at[j, i], sf_r.at[j, i], sib).wait_recv()

    some(8)
    from_far(0)
    some(8)
    from_far(1)
    some(4)
    from_near(0)
    from_far(2)
    some(4)
    from_near(1)
    from_far(3)
    from_sibling(0)
    own_in.wait()
    own_out.wait_recv()
    project_last()
    from_near(2)
    from_far(4)
    from_sibling(1)
    from_sibling(2)
    from_near(3)
    from_far(5)
    project(0)
    from_near(4)
    from_far(6)
    from_sibling(3)
    states(0)
    from_near(5)
    from_far(7)
    from_far(8)
    from_sibling(4)
    project(1)
    from_near(6)
    states(1)
    from_near(7)
    from_near(8)
    from_sibling(5)
    from_sibling(6)
    project(2)
    states(2)
    from_sibling(7)
    from_sibling(8)
    project(3)
    states(3)
    some(H)
    local_forward(0)
    local_forward(1)
    remote(
        tin.at[most], tin.at[most], tsem.at[0], tsem.at[1], sib
    ).wait_recv()
    tin[...] = jnp.exp(tin[...])

    def block(r):
        p = here
        for d in range(6):
            if (r >> d) & 1:
                p = flip(d, *p)
        return p[2] * 32 + p[1] * 8 + p[0] * 2 + p[3]

    def relay_tokens():
        tok_out.wait_recv()
        for r in range(64):
            b = block(r)
            ta[r] = tokt[core, b]
            tb[r] = ts[b]

    out_copy = pltpu.make_async_copy(outn, out_hbm, lsem.at[3])

    def give_output():
        for c in range(16):
            outn[:, 128 * c : 128 * c + 128] = outt[128 * c : 128 * c + 128, :].T
        out_copy.start()

    def close_affinity():
        ga = gaff[...].astype(BF)
        dct[...] += mm(xt[btall, :], ga, NN)
        dbt[...] += mm(xt[ctall, :], ga, NT)
        g[:, INNER + N : COLS] = dct[...].astype(BF).T

    def product(c, half):
        ids = order(c)[32 * half : 32 * half + 32]
        la = jnp.concatenate([ta[r] for r in ids], axis=0)
        lb = jnp.concatenate([tb[r] for r in ids], axis=0)
        cols = pl.ds(c * CW, CW)
        v = mm(la, g[:, cols], NN) + mm(lb, gs[:, cols], NN)
        return v.reshape(32, 16, CW).astype(BF)

    def halve(c, k):
        p = pl.ds(OFF[k], 32 >> k)
        return remote(sb.at[c, p], rb.at[c, p], wsem.at[c, k], wrsem.at[c, k], peers[(c + k) % 6])

    def direct(c, i):
        dims = [(c + 3 + b) % 6 for b in range(3) if (i >> (2 - b)) & 1]
        return remote(
            part.at[c, i], rb.at[c, OFF[3] + i - 1], wsem.at[c, 3], wrsem.at[c, 3], across(dims)
        )

    def first(c):
        sb[c, pl.ds(0, 32)] = product(c, 1)
        halve(c, 0).start()

    def tokens_part(i):
        r = pl.ds(512 * i, 512)
        tok[:, r] = mm(g[...], wf[r, :], NT).astype(BF)

    scan(0, 0, 0, 1)
    scan(0, 1, 0, 1)
    local_forward(2)
    scan(0, 2, 0, 1)
    mixture(0)
    local_forward(3)
    scan(0, 3, 0, 1)
    mixture(1)
    local_backward(0)
    mixture(2)
    scan(2, 0, 1, 0)
    local_backward(1)
    mixture(3)
    scan(2, 1, 1, 0)
    local_backward(2)
    give_output()
    scan(2, 2, 1, 0)
    local_backward(3)
    relay_tokens()
    finish(0)
    scan(2, 3, 1, 0)
    close_affinity()
    finish(1)
    g_copy(0).wait_recv()
    first(0)
    finish(2)
    g_copy(1).wait_recv()
    first(1)
    finish(3)
    g[:, INNER : INNER + N] = dbt[...].astype(BF).T
    g_copy(4).start()
    g_copy(2).wait_recv()
    first(2)
    first(3)
    g_copy(3).wait_recv()
    first(4)
    g_copy(4).wait_recv()
    first(5)
    for c in range(6):
        part[c] = product(c, 0)
    tokens_part(0)
    tokens_part(1)
    tokens_part(2)
    tokens_part(3)
    gt_copy = pltpu.make_async_copy(tok, gt_hbm, lsem.at[4])
    gt_copy.start()
    for k in range(1, 4):
        n = 64 >> k
        m = n // 2
        for c in range(6):
            halve(c, k - 1).wait_recv()
            if k < 3:
                sb[c, pl.ds(OFF[k], m)] = part[c, pl.ds(m, m)] + rb[c, pl.ds(OFF[k - 1] + m, m)]
                halve(c, k).start()
            else:
                part[c, pl.ds(0, n)] += rb[c, pl.ds(OFF[k - 1], n)]
                for i in range(7, 0, -1):
                    if c > 0:
                        direct(c - 1, i).start()
        if k == 3:
            for i in range(7, 0, -1):
                direct(5, i).start()
        if k < 3:
            for c in range(6):
                part[c, pl.ds(0, m)] += rb[c, pl.ds(OFF[k - 1], m)]
    rest = pl.ds(OFF[3], 7)
    for c in range(6):
        remote(rb.at[c, rest], rb.at[c, rest], wsem.at[c, 3], wrsem.at[c, 3], sib).wait_recv()
        v = part[c, 0].astype(F32)
        for i in range(7):
            v = v + rb[c, OFF[3] + i].astype(F32)
        gw_ref[:, pl.ds(c * CW, CW)] = v

    for i in range(PIECES):
        far_copy(i).wait_send()
        for d in range(3):
            near_copy(d, i).wait_send()
        for j in range(4):
            pass_copy(j, i).wait_send()
    own_out.wait_send()
    tok_out.wait_send()
    remote(tot.at[most], tot.at[most], tsem.at[0], tsem.at[1], sib).wait_send()
    for q in range(4):
        for k in range(4):
            left(k, q)
    for q in range(5):
        g_copy(q).wait_send()
    for c in range(6):
        for k in range(3):
            halve(c, k).wait_send()
        sent = pl.ds(1, 7)
        remote(
            part.at[c, sent], part.at[c, sent], wsem.at[c, 3], wrsem.at[c, 3], sib
        ).wait_send()
    out_copy.wait()
    gt_copy.wait()


def settle_kernel(a, b, c, a2, b2, c2):
    a2[...] = a[...]
    b2[...] = b[...]
    c2[...] = c[...]


def settle(*arrays):
    specs = [
        pl.BlockSpec((1, T // 2, INNER), lambda i: (0, i, 0)),
        pl.BlockSpec((1, T // 2, D), lambda i: (0, i, 0)),
        pl.BlockSpec((16, COLS // 2), lambda i: (0, i)),
    ]
    return pl.pallas_call(
        settle_kernel,
        name="settle",
        grid=(2,),
        out_shape=tuple(jax.ShapeDtypeStruct(v.shape, v.dtype) for v in arrays),
        in_specs=specs,
        out_specs=tuple(specs),
        compiler_params=pltpu.CompilerParams(vmem_limit_bytes=60 * 1024 * 1024),
    )(*arrays)


def on_device(tokens, w_in, log_decay, grad_out):
    v = pl.BlockSpec(memory_space=pltpu.VMEM)
    a = pl.BlockSpec(memory_space=pl.ANY)
    vm = pltpu.VMEM
    st = vm((4, 2, 32, 16, N), BF)
    sr = vm((4, 32, 2, 16, N), BF)
    dma = pltpu.SemaphoreType.DMA
    out, gt, gw = pl.pallas_call(
        kernel,
        name="mixer_step",
        out_shape=(
            jax.ShapeDtypeStruct((T, INNER), BF),
            jax.ShapeDtypeStruct((T, D), BF),
            jax.ShapeDtypeStruct((16, COLS), F32),
        ),
        in_specs=[a, a, v, a],
        out_specs=(a, a, v),
        scratch_shapes=[
            vm((D, COLS), BF),
            vm((T, D), BF),
            vm((2, 64, 16, T), BF),
            vm((64, 16, T), BF),
            vm((64, 16, T), BF),
            vm((64, 16, T), BF),
            vm((T, INNER), BF),
            vm((INNER, T), BF),
            vm((COLS, T), BF),
            vm((H, 8, T), F32),
            vm((H, 8, N), F32),
            vm((H, 8, N), F32),
            vm((H, T, T), BF),
            vm((T, T), BF),
            vm((H, PS, T), F32),
            vm((H, PS, T), BF),
            vm((H, 2 * PS, T), BF),
            vm((H, 2 * PS, T), BF),
            vm((T, T), F32),
            vm((N, T), F32),
            vm((N, T), F32),
            vm((T, N), BF),
            vm((T, N), BF),
            st, sr, sr, st, st, sr, sr, st,
            vm((INNER, T), BF),
            vm((T, INNER), BF),
            vm((INNER, T), BF),
            vm((T, COLS), BF),
            vm((T, COLS), BF),
            vm((6, 32, 16, CW), BF),
            vm((6, 63, 16, CW), BF),
            vm((6, 63, 16, CW), BF),
            dma((5,)),
            dma((PIECES,)),
            dma((PIECES,)),
            dma((3, PIECES)),
            dma((3, PIECES)),
            dma((4, PIECES)),
            dma((4, PIECES)),
            dma((2,)),
            dma((2,)),
            dma((5,)),
            dma((5,)),
            dma((4, 4)),
            dma((4, 4)),
            dma((2,)),
            dma((6, 4)),
            dma((6, 4)),
        ],
        compiler_params=pltpu.CompilerParams(
            collective_id=0, has_side_effects=True, vmem_limit_bytes=60 * 1024 * 1024
        ),
    )(tokens[0], w_in, log_decay[0], grad_out[0])
    return settle(out[None], gt[None], gw)


def solution(mesh):
    return jax.shard_map(
        on_device,
        mesh=mesh,
        in_specs=(
            P("fsdp", "seq", None),
            P("fsdp", None),
            P("fsdp", None, "seq"),
            P("fsdp", "seq", None),
        ),
        out_specs=(P("fsdp", "seq", None), P("fsdp", "seq", None), P(("seq", "fsdp"), None)),
        check_vma=False,
    )
```

```python
import functools
import jax
import jax.numpy as jnp
from jax import lax
from jax.experimental import pallas as pl
from jax.experimental.pallas import tpu as pltpu
from jax.sharding import PartitionSpec as P

BF = jnp.bfloat16
F32 = jnp.float32
EPS = 1e-5
H, PS, N, T, D, INNER, COLS = 32, 64, 128, 256, 2048, 2048, 2304
MESH = pl.DeviceIdType.MESH
NN = (((1,), (0,)), ((), ()))
NT = (((1,), (1,)), ((), ()))
TN = (((0,), (0,)), ((), ()))
CW = COLS // 6
OFF = [0, 32, 48, 56]
UNITS = [(c, 0, 256, 256 * c) for c in range(6)] + [(c, 256, 128, 1536 + 128 * c) for c in range(6)]
PIECES = 9
NEAR = 7
GROUP = 4


def mm(a, b, dims):
    return lax.dot_general(a, b, dims, preferred_element_type=F32)


def place():
    s = lax.axis_index("seq")
    f = lax.axis_index("fsdp")
    return s % 4, (s // 4) % 4, s // 16, f // 2, f % 2


def device(x, y, zl, zh, core):
    return (zl * 16 + y * 4 + x, zh * 2 + core)


def flip(dim, x, y, zl, zh):
    if dim == 0:
        x = x + 1 - 2 * (x % 2)
    elif dim == 1:
        x = 3 - x
    elif dim == 2:
        y = y + 1 - 2 * (y % 2)
    elif dim == 3:
        y = 3 - y
    elif dim == 4:
        zl = 1 - zl
    else:
        zl, zh = 1 - zl, 1 - zh
    return x, y, zl, zh


def order(color):
    dims = [(color + 5 + k) % 6 for k in range(6)]
    found = []
    for i in range(64):
        r = 0
        for k in range(6):
            if (i >> (5 - k)) & 1:
                r |= 1 << dims[k]
        found.append(r)
    return found


def remote(src, dst, ssem, rsem, to):
    return pltpu.make_async_remote_copy(src, dst, ssem, rsem, to, MESH)


def kernel(
    tok_hbm, w_hbm, log_ref, go_hbm,
    out_hbm, gt_hbm, gw_ref,
    wf, tok, tokt, ts, ta, tb, go, gtr, xt, rows, tot, tin,
    dec, aff, y, gm, gmw, xs, gaff, dct, dbt, bmat, cmat,
    up1, in1, down1, ent, up2, in2, down2, adj,
    outt, outn, grad, g, gs, part, sb, rb,
    lsem, far_s, far_r, nb_s, nb_r, sf_s, sf_r, sib_s, sib_r, gsib_s, gsib_r,
    ssem, rsem, tsem, wsem, wrsem,
):
    s = lax.axis_index("seq")
    f = lax.axis_index("fsdp")
    x, y_, zl, zh, core = place()
    here = (x, y_, zl, zh)
    sib = device(*here, 1 - core)
    far = device(*flip(5, *here), core)
    peers = [device(*flip(d, *here), core) for d in range(6)]
    barrier = pltpu.get_barrier_semaphore()

    pxs = [lax.rem(x + d, 4) for d in range(4)]
    pys = [4 * lax.rem(y_ + d, 4) for d in range(4)]
    pzs = [16 * lax.rem(zl + d, 2) for d in range(2)]
    pyz = [a + b for a in pzs for b in pys]
    ring = [pyz[o // 4] + pxs[o % 4] for o in range(1, 32)]

    for p in ring:
        pl.semaphore_signal(barrier, inc=1, device_id=(p, f), device_id_type=MESH)

    def across(dims):
        p = here
        for d in dims:
            p = flip(d, *p)
        return device(*p, core)

    further = [(3, 5), (4, 5), (3, 4, 5), (0, 5), (0, 4, 5), (1, 5), (0, 1, 5)]
    greeted = [sib, far] + [across(d) for d in further]
    for q in greeted:
        pl.semaphore_signal(barrier, inc=1, device_id=q, device_id_type=MESH)

    def whole(i):
        return pl.ds(pl.multiple_of(i * 512, 512), 512)

    tok_in = pltpu.make_async_copy(tok_hbm, tok, lsem.at[0])
    go_in = pltpu.make_async_copy(go_hbm, go, lsem.at[1])
    own_in = pltpu.make_async_copy(w_hbm, wf.at[whole(f)], lsem.at[2])
    tok_in.start()
    own_in.start()
    go_in.start()

    ri = lax.broadcasted_iota(jnp.int32, (T, T), 0)
    ci = lax.broadcasted_iota(jnp.int32, (T, T), 1)
    log = log_ref[...]
    cum = lax.dot_general(
        log, (ri <= ci).astype(F32), NN, precision=lax.Precision.HIGHEST, preferred_element_type=F32
    )
    exc = cum - log
    last = cum[:, T - 1 : T]
    cumt = cum.T
    exct = exc.T
    fac = (jnp.exp(cum), jnp.exp(last - exc), jnp.exp(last - cum), jnp.exp(exc))
    lastb = jnp.broadcast_to(last, (H, N))
    for h in range(H):
        for k in range(4):
            rows[h, k : k + 1, :] = fac[k][h : h + 1, :]
    for h in range(8):
        four = [lastb[8 * k + h : 8 * k + h + 1, :] for k in range(4)]
        v = jnp.concatenate(four + four, axis=0)
        for k in range(4):
            tot[4 * h + k] = v

    pl.semaphore_wait(barrier, 31 + len(greeted))

    far_f = (1 - zh) * 2 + core
    sibfar_f = (1 - zh) * 2 + 1 - core
    bits = [(x + x // 2) % 2, x // 2, (y_ + y_ // 2) % 2, y_ // 2, zl]

    def cover(i):
        dims = [(i + k) % 5 for k in range(3)]
        v = [bits[d] for d in dims]
        q0, q1 = (v[0] + v[2]) % 2, (v[1] + v[2]) % 2
        theirs = [(1 - q0) + 2 * q1, q0 + 2 * (1 - q1), (1 - q0) + 2 * (1 - q1)]
        mine = q0 + 2 * q1
        return dims, mine, theirs, theirs[dims.index(4)] if 4 in dims else mine

    covers = [cover(i) for i in range(PIECES)]

    def piece(shard, quarter, i):
        r = pl.ds(pl.multiple_of(shard * 512 + quarter * 128, 128), 128)
        return r, pl.ds(256 * ((i + 8) % 9), 256)

    def far_copy(i):
        if i >= NEAR:
            cols = piece(f, 0, i)[1]
            p = (whole(f), cols)
            return remote(w_hbm.at[:, cols], wf.at[p], far_s.at[i], far_r.at[i], far)
        quarter = covers[i][3]
        mine = pl.ds(pl.multiple_of(quarter * 128, 128), 128)
        p = piece(f, quarter, i)
        return remote(w_hbm.at[mine, p[1]], wf.at[p], far_s.at[i], far_r.at[i], far)

    def near_copy(d, i):
        p = piece(far_f, covers[i][1], i)
        return remote(wf.at[p], wf.at[p], nb_s.at[d, i], nb_r.at[d, i], peers[covers[i][0][d]])

    def pass_copy(j, i):
        p = piece(far_f, covers[i][1] if j == 0 else covers[i][2][j - 1], i)
        if i >= NEAR:
            p = (whole(far_f), p[1])
        return remote(wf.at[p], wf.at[p], sf_s.at[j, i], sf_r.at[j, i], sib)

    own_out = remote(w_hbm, wf.at[whole(f)], sib_s.at[0], sib_r.at[0], sib)
    for i in range(PIECES):
        far_copy(i).start()
    own_out.start()

    for p in ring:
        remote(tot.at[p], tin.at[s], tsem.at[0], tsem.at[1], (p, f)).start()

    tin[s] = tot[s]
    most = pl.ds(0, 31)

    diag = ri == ci

    def decays(h):
        a = cum[h : h + 1, :] - cumt[:, h : h + 1]
        b = exct[:, h : h + 1] - exc[h : h + 1, :]
        e = jnp.exp(jnp.minimum(a, b))
        dec[h] = jnp.where(diag, 2.0, e).astype(BF)

    tok_in.wait()
    for c in range(16):
        tt = tok[:, 128 * c : 128 * c + 128].T
        for k in range(8):
            b = 8 * c + k
            tokt[b % 2, b // 2] = tt[16 * k : 16 * k + 16, :]
    tok_out = remote(tokt.at[1 - core], ts, sib_s.at[1], sib_r.at[1], sib)
    tok_out.start()

    go_in.wait()
    for c in range(16):
        gtr[128 * c : 128 * c + 128, :] = go[:, 128 * c : 128 * c + 128].T

    def head(h):
        return pl.ds(pl.multiple_of(h * PS, PS), PS)

    def transfer(k, q, p):
        src, dst = ((up1, in1), (down1, ent), (up2, in2), (down2, adj))[k]
        a = src.at[q, p] if k % 2 else src.at[q, :, p]
        b = dst.at[q, :, s] if k % 2 else dst.at[q, s]
        return remote(a, b, ssem.at[k, q], rsem.at[k, q], (p, f))

    def send(k, q):
        src, dst = ((up1, in1), (down1, ent), (up2, in2), (down2, adj))[k]

        for p in ring:
            transfer(k, q, p).start()

        if k % 2:
            dst[q, :, s] = src[q, s]
        else:
            dst[q, s] = src[q, :, s]

    def whole_chunk(k, q):
        src, dst = ((up1, in1), (down1, ent), (up2, in2), (down2, adj))[k]
        a = src.at[q, most] if k % 2 else src.at[q, :, most]
        b = dst.at[q, :, most] if k % 2 else dst.at[q, most]
        return a, b

    def arrived(k, q):
        _, b = whole_chunk(k, q)
        remote(b, b, ssem.at[k, q], rsem.at[k, q], sib).wait_recv()

    def left(k, q):
        a, _ = whole_chunk(k, q)
        remote(a, a, ssem.at[k, q], rsem.at[k, q], sib).wait_send()

    def pairs(q, body):
        @pl.loop(0, 8 // GROUP)
        def _(t):
            body([(8 * q + GROUP * t + i, GROUP * t + i) for i in range(GROUP)])

    def quarter(ref, q, i):
        return jnp.concatenate(
            [ref[q, k, pl.ds(4 * i, 4)].reshape(PS, N) for k in range(2)], axis=0
        )

    def store(ref, q, i, v):
        v = v.reshape(2, 4, 16, N)
        for k in range(2):
            ref[q, k, pl.ds(4 * i, 4)] = v[k]

    ctall = pl.ds(INNER + N, N)
    btall = pl.ds(INNER, N)

    def project(q):
        cols = pl.ds(512 * q, 512)
        v = mm(tok[...], wf[:, cols], NN).astype(BF)
        for c in range(4):
            xt[512 * q + 128 * c : 512 * q + 128 * c + 128, :] = v[:, 128 * c : 128 * c + 128].T

    def project_last():
        v = mm(tok[...], wf[:, INNER:COLS], NN).astype(BF)
        bmat[...] = v[:, :N]
        cmat[...] = v[:, N:]
        xt[btall, :] = v[:, :N].T
        xt[ctall, :] = v[:, N:].T
        aff[...] = mm(v[:, :N], xt[ctall, :], NN).astype(BF)

    def states(q):
        def body(hs):
            for h, i in hs:
                xv = xt[head(h), :].astype(F32)
                r = rows[h]
                xs[h, pl.ds(0, PS), :] = (xv * r[2:3, :]).astype(BF)
                xs[h, pl.ds(PS, PS), :] = (xv * r[3:4, :]).astype(BF)
            for h, i in hs:
                store(up1, q, i, mm(xs[h], bmat[...], NN).astype(BF))

        pairs(q, body)
        send(0, q)

    def local_forward(q):
        def body(hs):
            for h, _ in hs:
                y[h] = mm(xt[head(h), :], aff[...] * dec[h], NN)

        pairs(q, body)

    def scan(k, q, fwd, rev):
        src, dst = ((in1, down1), None, (in2, down2))[k]
        arrived(k, q)

        def one(i, carry):
            a, b = carry
            j = 31 - i
            dst[q, i, fwd] = a.astype(BF)
            dst[q, j, rev] = b.astype(BF)
            a = tin[i, q : q + 1, :] * a + src[q, i, fwd].astype(F32)
            b = tin[j, q : q + 1, :] * b + src[q, j, rev].astype(F32)
            return a, b

        zero = jnp.zeros((16, N), F32)
        lax.fori_loop(0, 32, one, (zero, zero), unroll=32)
        send(k + 1, q)

    def mixture(q):
        arrived(1, q)

        def body(hs):
            for h, i in hs:
                r = rows[h]
                car = mm(quarter(ent, q, i), xt[ctall, :], NN)
                mix = y[h] + r[0:1, :] * car[:PS] + r[1:2, :] * car[PS:]
                ms = jnp.sum(mix * mix, axis=0, keepdims=True) * (1.0 / PS)
                inv = 1.0 / jnp.sqrt(ms + EPS)
                z = mix * inv
                outt[head(h), :] = z.astype(BF)
                gv = gtr[head(h), :].astype(F32)
                m = jnp.sum(gv * z, axis=0, keepdims=True) * (1.0 / PS)
                gr = (gv - z * m) * inv
                gm[h] = gr.astype(BF)
                gmw[h, pl.ds(0, PS), :] = (gr * r[0:1, :]).astype(BF)
                gmw[h, pl.ds(PS, PS), :] = (gr * r[1:2, :]).astype(BF)
            for h, i in hs:
                store(up2, q, i, mm(gmw[h], cmat[...], NN).astype(BF))

        pairs(q, body)
        send(2, q)

    def local_backward(q):
        def body(hs):
            total = None
            for h, i in hs:
                d = dec[h]
                gh = gm[h]
                y[h] = mm(gh, aff[...] * d, NT)
                gw = mm(xt[head(h), :], gh, TN) * d.astype(F32)
                total = gw if total is None else total + gw
            gaff[...] += total
            e = jnp.concatenate([quarter(ent, q, i) for _, i in hs], axis=0)
            w = jnp.concatenate([gmw[h] for h, _ in hs], axis=0)
            dct[...] += mm(e, w, TN)

        pairs(q, body)

    def finish(q):
        arrived(3, q)

        def body(hs):
            total = None
            for h, i in hs:
                r = rows[h]
                e = quarter(adj, q, i)
                car = mm(e, xt[btall, :], NN)
                gx = y[h] + r[2:3, :] * car[:PS] + r[3:4, :] * car[PS:]
                grad[head(h), :] = gx.astype(BF)
                v = mm(e, xs[h], TN)
                total = v if total is None else total + v
            dbt[...] += total

        pairs(q, body)
        for c in range(4 * q, 4 * q + 4):
            g[:, 128 * c : 128 * c + 128] = grad[128 * c : 128 * c + 128, :].T
        g_copy(q).start()

    def g_copy(q):
        cols = pl.ds(512 * q, 512 if q < 4 else 256)
        return remote(g.at[:, cols], gs.at[:, cols], gsib_s.at[q], gsib_r.at[q], sib)

    todo = list(range(H))

    def some(n):
        for h in todo[:n]:
            decays(h)
        del todo[:n]

    gaff[...] = jnp.zeros_like(gaff)
    dct[...] = jnp.zeros_like(dct)
    dbt[...] = jnp.zeros_like(dbt)
    def from_far(i):
        far_copy(i).wait_recv()
        for d in range(3 if i < NEAR else 0):
            near_copy(d, i).start()
        pass_copy(0, i).start()

    def from_near(i):
        for d in range(3):
            p = piece(far_f, covers[i][2][d], i)
            to = peers[covers[i][0][d]]
            remote(wf.at[p], wf.at[p], nb_s.at[d, i], nb_r.at[d, i], to).wait_recv()
            pass_copy(1 + d, i).start()

    def from_sibling(i):
        for j in range(4 if i < NEAR else 1):
            p = piece(sibfar_f, covers[i][1] if j == 0 else covers[i][2][j - 1], i)
            if i >= NEAR:
                p = (whole(sibfar_f), p[1])
            remote(wf.at[p], wf.at[p], sf_s.at[j, i], sf_r.at[j, i], sib).wait_recv()

    some(8)
    from_far(0)
    some(8)
    from_far(1)
    from_near(0)
    from_far(2)
    some(4)
    from_near(1)
    from_far(3)
    from_sibling(0)
    own_in.wait()
    own_out.wait_recv()
    project_last()
    from_near(2)
    from_far(4)
    from_sibling(1)
    from_far(5)
    from_near(3)
    from_sibling(2)
    project(0)
    from_far(6)
    from_near(4)
    states(0)
    from_near(5)
    from_sibling(3)
    from_sibling(4)
    project(1)
    from_near(6)
    states(1)
    some(4)
    from_sibling(5)
    from_sibling(6)
    from_far(7)
    project(2)
    states(2)
    from_far(8)
    from_sibling(7)
    from_sibling(8)
    project(3)
    states(3)
    some(H)
    local_forward(0)
    local_forward(1)
    remote(tin.at[most], tin.at[most], tsem.at[0], tsem.at[1], sib).wait_recv()
    tin[...] = jnp.exp(tin[...])
    scan(0, 0, 0, 1)

    def block(r):
        p = here
        for d in range(6):
            if (r >> d) & 1:
                p = flip(d, *p)
        return p[2] * 32 + p[1] * 8 + p[0] * 2 + p[3]

    def relay_tokens():
        tok_out.wait_recv()
        for r in range(64):
            b = block(r)
            ta[r] = tokt[core, b]
            tb[r] = ts[b]

    out_copy = pltpu.make_async_copy(outn, out_hbm, lsem.at[3])

    def give_output():
        for c in range(16):
            outn[:, 128 * c : 128 * c + 128] = outt[128 * c : 128 * c + 128, :].T
        out_copy.start()

    def close_affinity():
        ga = gaff[...].astype(BF)
        dct[...] += mm(xt[btall, :], ga, NN)
        dbt[...] += mm(xt[ctall, :], ga, NT)
        g[:, INNER + N : COLS] = dct[...].astype(BF).T

    def product(u, half):
        c, _, n, col = UNITS[u]
        ids = order(c)[32 * half : 32 * half + 32]
        la = jnp.concatenate([ta[r] for r in ids], axis=0)
        lb = jnp.concatenate([tb[r] for r in ids], axis=0)
        cols = pl.ds(col, n)
        v = mm(la, g[:, cols], NN) + mm(lb, gs[:, cols], NN)
        return v.reshape(32, 16, n).astype(BF)

    def lanes(u):
        return pl.ds(UNITS[u][1], UNITS[u][2])

    def halve(u, k):
        c = UNITS[u][0]
        p = (c, pl.ds(OFF[k], 32 >> k), slice(None), lanes(u))
        return remote(sb.at[p], rb.at[p], wsem.at[u, k], wrsem.at[u, k], peers[(c + 5 + k) % 6])

    def direct(u, i):
        c = UNITS[u][0]
        dims = [(c + 8 + b) % 6 for b in range(3) if (i >> (2 - b)) & 1]
        return remote(
            part.at[c, i, :, lanes(u)], rb.at[c, OFF[3] + i - 1, :, lanes(u)],
            wsem.at[u, 3], wrsem.at[u, 3], across(dims),
        )

    def first(*units):
        for u in units:
            sb[UNITS[u][0], pl.ds(0, 32), :, lanes(u)] = product(u, 1)
            halve(u, 0).start()

    def keep(*units):
        for u in units:
            part[UNITS[u][0], pl.ds(0, 32), :, lanes(u)] = product(u, 0)

    def step(k, *units):
        n = 64 >> k
        m = n // 2
        for u in units:
            c, w = UNITS[u][0], lanes(u)
            halve(u, k - 1).wait_recv()
            if k < 3:
                got = rb[c, pl.ds(OFF[k - 1] + m, m), :, w]
                sb[c, pl.ds(OFF[k], m), :, w] = part[c, pl.ds(m, m), :, w] + got
                halve(u, k).start()
                part[c, pl.ds(0, m), :, w] += rb[c, pl.ds(OFF[k - 1], m), :, w]
            else:
                part[c, pl.ds(0, n), :, w] += rb[c, pl.ds(OFF[k - 1], n), :, w]
        if k == 3:
            for u in units:
                for i in range(7, 0, -1):
                    direct(u, i).start()

    def last_step(*units):
        for u in units:
            c, w = UNITS[u][0], lanes(u)
            p = rb.at[c, pl.ds(OFF[3], 7), :, w]
            remote(p, p, wsem.at[u, 3], wrsem.at[u, 3], sib).wait_recv()
            v = part[c, 0, :, w].astype(F32)
            for i in range(7):
                v = v + rb[c, OFF[3] + i, :, w].astype(F32)
            gw_ref[:, pl.ds(UNITS[u][3], UNITS[u][2])] = v

    def tokens_part(i):
        r = pl.ds(512 * i, 512)
        tok[:, r] = mm(g[...], wf[r, :], NT).astype(BF)

    scan(0, 1, 0, 1)
    local_forward(2)
    scan(0, 2, 0, 1)
    mixture(0)
    local_forward(3)
    scan(0, 3, 0, 1)
    mixture(1)
    local_backward(0)
    mixture(2)
    scan(2, 0, 1, 0)
    local_backward(1)
    mixture(3)
    scan(2, 1, 1, 0)
    local_backward(2)
    relay_tokens()
    finish(0)
    scan(2, 2, 1, 0)
    local_backward(3)
    g_copy(0).wait_recv()
    first(0, 1)
    finish(1)
    scan(2, 3, 1, 0)
    close_affinity()
    keep(0, 1)
    g_copy(1).wait_recv()
    first(2, 3)
    give_output()
    keep(2, 3)
    finish(2)
    step(1, 0, 1)
    g_copy(2).wait_recv()
    first(4, 5)
    finish(3)
    g[:, INNER : INNER + N] = dbt[...].astype(BF).T
    g_copy(4).start()
    g_copy(3).wait_recv()
    first(6, 7, 8, 9)
    g_copy(4).wait_recv()
    first(10, 11)
    step(1, 2, 3)
    keep(4, 5)
    keep(6, 7, 8, 9, 10, 11)
    step(2, 0, 1)
    tokens_part(0)
    tokens_part(1)
    step(1, 4, 5)
    step(1, 6, 7, 8, 9, 10, 11)
    tokens_part(2)
    step(2, 2, 3)
    step(3, 0, 1)
    tokens_part(3)
    gt_copy = pltpu.make_async_copy(tok, gt_hbm, lsem.at[4])
    gt_copy.start()
    step(2, 4, 5)
    step(2, 6, 7, 8, 9, 10, 11)
    step(3, 2, 3)
    step(3, 4, 5)
    step(3, 6, 7, 8, 9, 10, 11)
    last_step(0, 1, 2, 3, 4, 5, 6, 7, 8, 9, 10, 11)

    for i in range(PIECES):
        far_copy(i).wait_send()
        for d in range(3 if i < NEAR else 0):
            near_copy(d, i).wait_send()
        for j in range(4 if i < NEAR else 1):
            pass_copy(j, i).wait_send()
    own_out.wait_send()
    tok_out.wait_send()
    remote(tot.at[most], tot.at[most], tsem.at[0], tsem.at[1], sib).wait_send()
    for q in range(4):
        for k in range(4):
            left(k, q)
    for q in range(5):
        g_copy(q).wait_send()
    for u in range(12):
        for k in range(3):
            halve(u, k).wait_send()
        p = part.at[UNITS[u][0], pl.ds(1, 7), :, lanes(u)]
        remote(p, p, wsem.at[u, 3], wrsem.at[u, 3], sib).wait_send()
    out_copy.wait()
    gt_copy.wait()


def settle_kernel(a, b, c, a2, b2, c2, va, vb, vc, sem):
    moves = [(a.at[0, pl.ds(64 * i, 64)], va.at[pl.ds(64 * i, 64)], a2.at[0, pl.ds(64 * i, 64)]) for i in range(4)]
    moves += [(b.at[0, pl.ds(64 * i, 64)], vb.at[pl.ds(64 * i, 64)], b2.at[0, pl.ds(64 * i, 64)]) for i in range(4)]
    moves.append((c, vc, c2))
    ins = [pltpu.make_async_copy(m[0], m[1], sem.at[0, i]) for i, m in enumerate(moves)]
    outs = [pltpu.make_async_copy(m[1], m[2], sem.at[1, i]) for i, m in enumerate(moves)]
    for m in ins:
        m.start()
    for m, n in zip(ins, outs):
        m.wait()
        n.start()
    for n in outs:
        n.wait()


def settle(*arrays):
    v = pl.BlockSpec(memory_space=pl.ANY)
    return pl.pallas_call(
        settle_kernel,
        name="settle",
        out_shape=tuple(jax.ShapeDtypeStruct(v.shape, v.dtype) for v in arrays),
        in_specs=[v] * 3,
        out_specs=(v,) * 3,
        scratch_shapes=[
            pltpu.VMEM((T, INNER), BF),
            pltpu.VMEM((T, D), BF),
            pltpu.VMEM((16, COLS), F32),
            pltpu.SemaphoreType.DMA((2, 9)),
        ],
        compiler_params=pltpu.CompilerParams(vmem_limit_bytes=60 * 1024 * 1024),
    )(*arrays)


def on_device(tokens, w_in, log_decay, grad_out):
    v = pl.BlockSpec(memory_space=pltpu.VMEM)
    a = pl.BlockSpec(memory_space=pl.ANY)
    vm = pltpu.VMEM
    st = vm((4, 2, 32, 16, N), BF)
    sr = vm((4, 32, 2, 16, N), BF)
    dma = pltpu.SemaphoreType.DMA
    out, gt, gw = pl.pallas_call(
        kernel,
        name="mixer_step",
        out_shape=(
            jax.ShapeDtypeStruct((T, INNER), BF),
            jax.ShapeDtypeStruct((T, D), BF),
            jax.ShapeDtypeStruct((16, COLS), F32),
        ),
        in_specs=[a, a, v, a],
        out_specs=(a, a, v),
        scratch_shapes=[
            vm((D, COLS), BF),
            vm((T, D), BF),
            vm((2, 64, 16, T), BF),
            vm((64, 16, T), BF),
            vm((64, 16, T), BF),
            vm((64, 16, T), BF),
            vm((T, INNER), BF),
            vm((INNER, T), BF),
            vm((COLS, T), BF),
            vm((H, 8, T), F32),
            vm((H, 8, N), F32),
            vm((H, 8, N), F32),
            vm((H, T, T), BF),
            vm((T, T), BF),
            vm((H, PS, T), F32),
            vm((H, PS, T), BF),
            vm((H, 2 * PS, T), BF),
            vm((H, 2 * PS, T), BF),
            vm((T, T), F32),
            vm((N, T), F32),
            vm((N, T), F32),
            vm((T, N), BF),
            vm((T, N), BF),
            st, sr, sr, st, st, sr, sr, st,
            vm((INNER, T), BF),
            vm((T, INNER), BF),
            vm((INNER, T), BF),
            vm((T, COLS), BF),
            vm((T, COLS), BF),
            vm((6, 32, 16, CW), BF),
            vm((6, 63, 16, CW), BF),
            vm((6, 63, 16, CW), BF),
            dma((5,)),
            dma((PIECES,)),
            dma((PIECES,)),
            dma((3, PIECES)),
            dma((3, PIECES)),
            dma((4, PIECES)),
            dma((4, PIECES)),
            dma((2,)),
            dma((2,)),
            dma((5,)),
            dma((5,)),
            dma((4, 4)),
            dma((4, 4)),
            dma((2,)),
            dma((12, 4)),
            dma((12, 4)),
        ],
        compiler_params=pltpu.CompilerParams(
            collective_id=0, has_side_effects=True, vmem_limit_bytes=60 * 1024 * 1024
        ),
    )(tokens[0], w_in, log_decay[0], grad_out[0])
    return settle(out[None], gt[None], gw)


def solution(mesh):
    return jax.shard_map(
        on_device,
        mesh=mesh,
        in_specs=(
            P("fsdp", "seq", None),
            P("fsdp", None),
            P("fsdp", None, "seq"),
            P("fsdp", "seq", None),
        ),
        out_specs=(P("fsdp", "seq", None), P("fsdp", "seq", None), P(("seq", "fsdp"), None)),
        check_vma=False,
    )
```

```python
import functools
import jax
import jax.numpy as jnp
from jax import lax
from jax.experimental import pallas as pl
from jax.experimental.pallas import tpu as pltpu
from jax.sharding import PartitionSpec as P

BF = jnp.bfloat16
F32 = jnp.float32
EPS = 1e-5
H, PS, N, T, D, INNER, COLS = 32, 64, 128, 256, 2048, 2048, 2304
MESH = pl.DeviceIdType.MESH
NN = (((1,), (0,)), ((), ()))
NT = (((1,), (1,)), ((), ()))
TN = (((0,), (0,)), ((), ()))
CW = COLS // 6
OFF = [0, 32, 48, 56]
UNITS = [(c, 0, 256, 256 * c) for c in range(6)] + [(c, 256, 128, 1536 + 128 * c) for c in range(6)]
PIECES = 9
NEAR = 7
GROUP = 4


def mm(a, b, dims):
    return lax.dot_general(a, b, dims, preferred_element_type=F32)


def place():
    s = lax.axis_index("seq")
    f = lax.axis_index("fsdp")
    return s % 4, (s // 4) % 4, s // 16, f // 2, f % 2


def device(x, y, zl, zh, core):
    return (zl * 16 + y * 4 + x, zh * 2 + core)


def flip(dim, x, y, zl, zh):
    if dim == 0:
        x = x + 1 - 2 * (x % 2)
    elif dim == 1:
        x = 3 - x
    elif dim == 2:
        y = y + 1 - 2 * (y % 2)
    elif dim == 3:
        y = 3 - y
    elif dim == 4:
        zl = 1 - zl
    else:
        zl, zh = 1 - zl, 1 - zh
    return x, y, zl, zh


def order(color):
    dims = [(color + 5 + k) % 6 for k in range(6)]
    found = []
    for i in range(64):
        r = 0
        for k in range(6):
            if (i >> (5 - k)) & 1:
                r |= 1 << dims[k]
        found.append(r)
    return found


def remote(src, dst, ssem, rsem, to):
    return pltpu.make_async_remote_copy(src, dst, ssem, rsem, to, MESH)


def kernel(
    tok_hbm, w_hbm, log_ref, go_hbm,
    out_hbm, gt_hbm, gw_ref,
    wf, tok, tokt, ts, ta, tb, go, gtr, xt, rows, tot, tin,
    dec, aff, y, gm, gmw, xs, gaff, dct, dbt, bmat, cmat,
    up1, in1, down1, ent, up2, in2, down2, adj,
    outt, outn, grad, g, gs, part, sb, rb,
    lsem, far_s, far_r, nb_s, nb_r, sf_s, sf_r, sib_s, sib_r, gsib_s, gsib_r,
    ssem, rsem, tsem, wsem, wrsem,
):
    s = lax.axis_index("seq")
    f = lax.axis_index("fsdp")
    x, y_, zl, zh, core = place()
    here = (x, y_, zl, zh)
    sib = device(*here, 1 - core)
    far = device(*flip(5, *here), core)
    peers = [device(*flip(d, *here), core) for d in range(6)]
    barrier = pltpu.get_barrier_semaphore()

    pxs = [lax.rem(x + d, 4) for d in range(4)]
    pys = [4 * lax.rem(y_ + d, 4) for d in range(4)]
    pzs = [16 * lax.rem(zl + d, 2) for d in range(2)]
    pyz = [a + b for a in pzs for b in pys]
    ring = [pzs[o // 16] + pys[o % 4] + pxs[(o // 4) % 4] for o in range(1, 32)]

    for p in ring:
        pl.semaphore_signal(barrier, inc=1, device_id=(p, f), device_id_type=MESH)

    def across(dims):
        p = here
        for d in dims:
            p = flip(d, *p)
        return device(*p, core)

    further = [(3, 5), (4, 5), (3, 4, 5), (0, 5), (0, 4, 5), (1, 5), (0, 1, 5)]
    greeted = [sib, far] + [across(d) for d in further]
    for q in greeted:
        pl.semaphore_signal(barrier, inc=1, device_id=q, device_id_type=MESH)

    def whole(i):
        return pl.ds(pl.multiple_of(i * 512, 512), 512)

    tok_in = pltpu.make_async_copy(tok_hbm, tok, lsem.at[0])
    go_in = pltpu.make_async_copy(go_hbm, go, lsem.at[1])
    own_in = pltpu.make_async_copy(w_hbm, wf.at[whole(f)], lsem.at[2])
    tok_in.start()
    own_in.start()
    go_in.start()

    ri = lax.broadcasted_iota(jnp.int32, (T, T), 0)
    ci = lax.broadcasted_iota(jnp.int32, (T, T), 1)
    log = log_ref[...]
    cum = lax.dot_general(
        log, (ri <= ci).astype(F32), NN, precision=lax.Precision.HIGHEST, preferred_element_type=F32
    )
    exc = cum - log
    last = cum[:, T - 1 : T]
    cumt = cum.T
    exct = exc.T
    fac = (jnp.exp(cum), jnp.exp(last - exc), jnp.exp(last - cum), jnp.exp(exc))
    lastb = jnp.broadcast_to(last, (H, N))
    for h in range(H):
        for k in range(4):
            rows[h, k : k + 1, :] = fac[k][h : h + 1, :]
    for h in range(8):
        four = [lastb[8 * k + h : 8 * k + h + 1, :] for k in range(4)]
        v = jnp.concatenate(four + four, axis=0)
        for k in range(4):
            tot[4 * h + k] = v

    pl.semaphore_wait(barrier, 31 + len(greeted))

    far_f = (1 - zh) * 2 + core
    sibfar_f = (1 - zh) * 2 + 1 - core
    bits = [(x + x // 2) % 2, x // 2, (y_ + y_ // 2) % 2, y_ // 2, zl]

    def cover(i):
        dims = [(i + k) % 5 for k in range(3)]
        v = [bits[d] for d in dims]
        q0, q1 = (v[0] + v[2]) % 2, (v[1] + v[2]) % 2
        theirs = [(1 - q0) + 2 * q1, q0 + 2 * (1 - q1), (1 - q0) + 2 * (1 - q1)]
        mine = q0 + 2 * q1
        return dims, mine, theirs, theirs[dims.index(4)] if 4 in dims else mine

    covers = [cover(i) for i in range(PIECES)]

    def piece(shard, quarter, i):
        r = pl.ds(pl.multiple_of(shard * 512 + quarter * 128, 128), 128)
        return r, pl.ds(256 * ((i + 8) % 9), 256)

    def far_copy(i):
        if i >= NEAR:
            cols = piece(f, 0, i)[1]
            p = (whole(f), cols)
            return remote(w_hbm.at[:, cols], wf.at[p], far_s.at[i], far_r.at[i], far)
        quarter = covers[i][3]
        mine = pl.ds(pl.multiple_of(quarter * 128, 128), 128)
        p = piece(f, quarter, i)
        return remote(w_hbm.at[mine, p[1]], wf.at[p], far_s.at[i], far_r.at[i], far)

    def near_copy(d, i):
        p = piece(far_f, covers[i][1], i)
        return remote(wf.at[p], wf.at[p], nb_s.at[d, i], nb_r.at[d, i], peers[covers[i][0][d]])

    def pass_copy(j, i):
        p = piece(far_f, covers[i][1] if j == 0 else covers[i][2][j - 1], i)
        if i >= NEAR:
            p = (whole(far_f), p[1])
        return remote(wf.at[p], wf.at[p], sf_s.at[j, i], sf_r.at[j, i], sib)

    own_out = remote(w_hbm, wf.at[whole(f)], sib_s.at[0], sib_r.at[0], sib)
    for i in range(PIECES):
        far_copy(i).start()
    own_out.start()

    for p in ring:
        remote(tot.at[p], tin.at[s], tsem.at[0], tsem.at[1], (p, f)).start()

    tin[s] = tot[s]
    most = pl.ds(0, 31)

    diag = ri == ci

    def decays(h):
        a = cum[h : h + 1, :] - cumt[:, h : h + 1]
        b = exct[:, h : h + 1] - exc[h : h + 1, :]
        e = jnp.exp(jnp.minimum(a, b))
        dec[h] = jnp.where(diag, 2.0, e).astype(BF)

    tok_in.wait()
    for c in range(16):
        tt = tok[:, 128 * c : 128 * c + 128].T
        for k in range(8):
            b = 8 * c + k
            tokt[b % 2, b // 2] = tt[16 * k : 16 * k + 16, :]
    tok_out = remote(tokt.at[1 - core], ts, sib_s.at[1], sib_r.at[1], sib)
    tok_out.start()

    go_in.wait()
    for c in range(16):
        gtr[128 * c : 128 * c + 128, :] = go[:, 128 * c : 128 * c + 128].T

    def head(h):
        return pl.ds(pl.multiple_of(h * PS, PS), PS)

    def transfer(k, q, p):
        src, dst = ((up1, in1), (down1, ent), (up2, in2), (down2, adj))[k]
        a = src.at[q, p] if k % 2 else src.at[q, :, p]
        b = dst.at[q, :, s] if k % 2 else dst.at[q, s]
        return remote(a, b, ssem.at[k, q], rsem.at[k, q], (p, f))

    def send(k, q):
        src, dst = ((up1, in1), (down1, ent), (up2, in2), (down2, adj))[k]

        for p in ring:
            transfer(k, q, p).start()

        if k % 2:
            dst[q, :, s] = src[q, s]
        else:
            dst[q, s] = src[q, :, s]

    def whole_chunk(k, q):
        src, dst = ((up1, in1), (down1, ent), (up2, in2), (down2, adj))[k]
        a = src.at[q, most] if k % 2 else src.at[q, :, most]
        b = dst.at[q, :, most] if k % 2 else dst.at[q, most]
        return a, b

    def arrived(k, q):
        _, b = whole_chunk(k, q)
        remote(b, b, ssem.at[k, q], rsem.at[k, q], sib).wait_recv()

    def left(k, q):
        a, _ = whole_chunk(k, q)
        remote(a, a, ssem.at[k, q], rsem.at[k, q], sib).wait_send()

    def pairs(q, body):
        @pl.loop(0, 8 // GROUP)
        def _(t):
            body([(8 * q + GROUP * t + i, GROUP * t + i) for i in range(GROUP)])

    def quarter(ref, q, i):
        return jnp.concatenate(
            [ref[q, k, pl.ds(4 * i, 4)].reshape(PS, N) for k in range(2)], axis=0
        )

    def store(ref, q, i, v):
        v = v.reshape(2, 4, 16, N)
        for k in range(2):
            ref[q, k, pl.ds(4 * i, 4)] = v[k]

    ctall = pl.ds(INNER + N, N)
    btall = pl.ds(INNER, N)

    def project(q):
        cols = pl.ds(512 * q, 512)
        v = mm(tok[...], wf[:, cols], NN).astype(BF)
        for c in range(4):
            xt[512 * q + 128 * c : 512 * q + 128 * c + 128, :] = v[:, 128 * c : 128 * c + 128].T

    def project_last():
        v = mm(tok[...], wf[:, INNER:COLS], NN).astype(BF)
        bmat[...] = v[:, :N]
        cmat[...] = v[:, N:]
        xt[btall, :] = v[:, :N].T
        xt[ctall, :] = v[:, N:].T
        aff[...] = mm(v[:, :N], xt[ctall, :], NN).astype(BF)

    def states(q):
        def body(hs):
            for h, i in hs:
                xv = xt[head(h), :].astype(F32)
                r = rows[h]
                xs[h, pl.ds(0, PS), :] = (xv * r[2:3, :]).astype(BF)
                xs[h, pl.ds(PS, PS), :] = (xv * r[3:4, :]).astype(BF)
            for h, i in hs:
                store(up1, q, i, mm(xs[h], bmat[...], NN).astype(BF))

        pairs(q, body)
        send(0, q)

    def local_forward(q):
        def body(hs):
            for h, _ in hs:
                y[h] = mm(xt[head(h), :], aff[...] * dec[h], NN)

        pairs(q, body)

    def scan(k, q, fwd, rev):
        src, dst = ((in1, down1), None, (in2, down2))[k]
        arrived(k, q)

        def one(i, carry):
            a, b = carry
            j = 31 - i
            dst[q, i, fwd] = a.astype(BF)
            dst[q, j, rev] = b.astype(BF)
            a = tin[i, q : q + 1, :] * a + src[q, i, fwd].astype(F32)
            b = tin[j, q : q + 1, :] * b + src[q, j, rev].astype(F32)
            return a, b

        zero = jnp.zeros((16, N), F32)
        lax.fori_loop(0, 32, one, (zero, zero), unroll=32)
        send(k + 1, q)

    def mixture(q):
        arrived(1, q)

        def body(hs):
            for h, i in hs:
                r = rows[h]
                car = mm(quarter(ent, q, i), xt[ctall, :], NN)
                mix = y[h] + r[0:1, :] * car[:PS] + r[1:2, :] * car[PS:]
                ms = jnp.sum(mix * mix, axis=0, keepdims=True) * (1.0 / PS)
                inv = 1.0 / jnp.sqrt(ms + EPS)
                z = mix * inv
                outt[head(h), :] = z.astype(BF)
                gv = gtr[head(h), :].astype(F32)
                m = jnp.sum(gv * z, axis=0, keepdims=True) * (1.0 / PS)
                gr = (gv - z * m) * inv
                gm[h] = gr.astype(BF)
                gmw[h, pl.ds(0, PS), :] = (gr * r[0:1, :]).astype(BF)
                gmw[h, pl.ds(PS, PS), :] = (gr * r[1:2, :]).astype(BF)
            for h, i in hs:
                store(up2, q, i, mm(gmw[h], cmat[...], NN).astype(BF))

        pairs(q, body)
        send(2, q)

    def local_backward(q):
        def body(hs):
            total = None
            for h, i in hs:
                d = dec[h]
                gh = gm[h]
                y[h] = mm(gh, aff[...] * d, NT)
                gw = mm(xt[head(h), :], gh, TN) * d.astype(F32)
                total = gw if total is None else total + gw
            gaff[...] += total
            e = jnp.concatenate([quarter(ent, q, i) for _, i in hs], axis=0)
            w = jnp.concatenate([gmw[h] for h, _ in hs], axis=0)
            dct[...] += mm(e, w, TN)

        pairs(q, body)

    def finish(q):
        arrived(3, q)

        def body(hs):
            total = None
            for h, i in hs:
                r = rows[h]
                e = quarter(adj, q, i)
                car = mm(e, xt[btall, :], NN)
                gx = y[h] + r[2:3, :] * car[:PS] + r[3:4, :] * car[PS:]
                grad[head(h), :] = gx.astype(BF)
                v = mm(e, xs[h], TN)
                total = v if total is None else total + v
            dbt[...] += total

        pairs(q, body)
        for c in range(4 * q, 4 * q + 4):
            g[:, 128 * c : 128 * c + 128] = grad[128 * c : 128 * c + 128, :].T
        g_copy(q).start()

    def g_copy(q):
        cols = pl.ds(512 * q, 512 if q < 4 else 256)
        return remote(g.at[:, cols], gs.at[:, cols], gsib_s.at[q], gsib_r.at[q], sib)

    todo = list(range(H))

    def some(n):
        for h in todo[:n]:
            decays(h)
        del todo[:n]

    gaff[...] = jnp.zeros_like(gaff)
    dct[...] = jnp.zeros_like(dct)
    dbt[...] = jnp.zeros_like(dbt)
    def from_far(i):
        far_copy(i).wait_recv()
        for d in range(3 if i < NEAR else 0):
            near_copy(d, i).start()
        pass_copy(0, i).start()

    def from_near(i):
        for d in range(3):
            p = piece(far_f, covers[i][2][d], i)
            to = peers[covers[i][0][d]]
            remote(wf.at[p], wf.at[p], nb_s.at[d, i], nb_r.at[d, i], to).wait_recv()
            pass_copy(1 + d, i).start()

    def from_sibling(i):
        for j in range(4 if i < NEAR else 1):
            p = piece(sibfar_f, covers[i][1] if j == 0 else covers[i][2][j - 1], i)
            if i >= NEAR:
                p = (whole(sibfar_f), p[1])
            remote(wf.at[p], wf.at[p], sf_s.at[j, i], sf_r.at[j, i], sib).wait_recv()

    some(8)
    from_far(0)
    some(8)
    from_far(1)
    from_near(0)
    from_far(2)
    some(4)
    from_near(1)
    from_far(3)
    from_sibling(0)
    own_in.wait()
    own_out.wait_recv()
    project_last()
    from_near(2)
    from_far(4)
    from_sibling(1)
    from_far(5)
    from_near(3)
    from_sibling(2)
    project(0)
    from_far(6)
    from_near(4)
    states(0)
    from_near(5)
    from_sibling(3)
    from_sibling(4)
    project(1)
    from_near(6)
    states(1)
    some(4)
    from_sibling(5)
    from_sibling(6)
    from_far(7)
    project(2)
    states(2)
    from_far(8)
    from_sibling(7)
    from_sibling(8)
    project(3)
    states(3)
    some(H)
    local_forward(0)
    local_forward(1)
    remote(tin.at[most], tin.at[most], tsem.at[0], tsem.at[1], sib).wait_recv()
    tin[...] = jnp.exp(tin[...])
    scan(0, 0, 0, 1)

    def block(r):
        p = here
        for d in range(6):
            if (r >> d) & 1:
                p = flip(d, *p)
        return p[2] * 32 + p[1] * 8 + p[0] * 2 + p[3]

    def relay_tokens():
        tok_out.wait_recv()
        for r in range(64):
            b = block(r)
            ta[r] = tokt[core, b]
            tb[r] = ts[b]

    out_copy = pltpu.make_async_copy(outn, out_hbm, lsem.at[3])

    def give_output():
        for c in range(16):
            outn[:, 128 * c : 128 * c + 128] = outt[128 * c : 128 * c + 128, :].T
        out_copy.start()

    def close_affinity():
        ga = gaff[...].astype(BF)
        dct[...] += mm(xt[btall, :], ga, NN)
        dbt[...] += mm(xt[ctall, :], ga, NT)
        g[:, INNER + N : COLS] = dct[...].astype(BF).T

    def product(u, half):
        c, _, n, col = UNITS[u]
        ids = order(c)[32 * half : 32 * half + 32]
        la = jnp.concatenate([ta[r] for r in ids], axis=0)
        lb = jnp.concatenate([tb[r] for r in ids], axis=0)
        cols = pl.ds(col, n)
        v = mm(la, g[:, cols], NN) + mm(lb, gs[:, cols], NN)
        return v.reshape(32, 16, n).astype(BF)

    def lanes(u):
        return pl.ds(UNITS[u][1], UNITS[u][2])

    def halve(u, k):
        c = UNITS[u][0]
        p = (c, pl.ds(OFF[k], 32 >> k), slice(None), lanes(u))
        return remote(sb.at[p], rb.at[p], wsem.at[u, k], wrsem.at[u, k], peers[(c + 5 + k) % 6])

    def direct(u, i):
        c = UNITS[u][0]
        dims = [(c + 8 + b) % 6 for b in range(3) if (i >> (2 - b)) & 1]
        return remote(
            part.at[c, i, :, lanes(u)], rb.at[c, OFF[3] + i - 1, :, lanes(u)],
            wsem.at[u, 3], wrsem.at[u, 3], across(dims),
        )

    def first(*units):
        for u in units:
            sb[UNITS[u][0], pl.ds(0, 32), :, lanes(u)] = product(u, 1)
            halve(u, 0).start()

    def keep(*units):
        for u in units:
            part[UNITS[u][0], pl.ds(0, 32), :, lanes(u)] = product(u, 0)

    def step(k, *units):
        n = 64 >> k
        m = n // 2
        for u in units:
            c, w = UNITS[u][0], lanes(u)
            halve(u, k - 1).wait_recv()
            if k < 3:
                got = rb[c, pl.ds(OFF[k - 1] + m, m), :, w]
                sb[c, pl.ds(OFF[k], m), :, w] = part[c, pl.ds(m, m), :, w] + got
                halve(u, k).start()
                part[c, pl.ds(0, m), :, w] += rb[c, pl.ds(OFF[k - 1], m), :, w]
            else:
                part[c, pl.ds(0, n), :, w] += rb[c, pl.ds(OFF[k - 1], n), :, w]
        if k == 3:
            for u in units:
                for i in range(7, 0, -1):
                    direct(u, i).start()

    def last_step(*units):
        for u in units:
            c, w = UNITS[u][0], lanes(u)
            p = rb.at[c, pl.ds(OFF[3], 7), :, w]
            remote(p, p, wsem.at[u, 3], wrsem.at[u, 3], sib).wait_recv()
            v = part[c, 0, :, w].astype(F32)
            for i in range(7):
                v = v + rb[c, OFF[3] + i, :, w].astype(F32)
            gw_ref[:, pl.ds(UNITS[u][3], UNITS[u][2])] = v

    def tokens_part(i):
        r = pl.ds(512 * i, 512)
        tok[:, r] = mm(g[...], wf[r, :], NT).astype(BF)

    scan(0, 1, 0, 1)
    local_forward(2)
    scan(0, 2, 0, 1)
    mixture(0)
    local_forward(3)
    scan(0, 3, 0, 1)
    mixture(1)
    local_backward(0)
    mixture(2)
    scan(2, 0, 1, 0)
    local_backward(1)
    mixture(3)
    scan(2, 1, 1, 0)
    local_backward(2)
    relay_tokens()
    finish(0)
    scan(2, 2, 1, 0)
    local_backward(3)
    scan(2, 3, 1, 0)
    close_affinity()
    g_copy(0).wait_recv()
    first(0)
    keep(0)
    finish(1)
    first(1)
    keep(1)
    give_output()
    g_copy(1).wait_recv()
    first(2, 3)
    keep(2, 3)
    finish(2)
    step(1, 0, 1)
    g_copy(2).wait_recv()
    first(4, 5)
    finish(3)
    g[:, INNER : INNER + N] = dbt[...].astype(BF).T
    g_copy(4).start()
    g_copy(3).wait_recv()
    first(6, 7, 8, 9)
    g_copy(4).wait_recv()
    first(10, 11)
    step(1, 2, 3)
    keep(4, 5)
    keep(6, 7, 8, 9, 10, 11)
    step(2, 0, 1)
    tokens_part(0)
    tokens_part(1)
    step(1, 4, 5)
    step(1, 6, 7, 8, 9, 10, 11)
    tokens_part(2)
    step(2, 2, 3)
    step(3, 0, 1)
    tokens_part(3)
    gt_copy = pltpu.make_async_copy(tok, gt_hbm, lsem.at[4])
    gt_copy.start()
    step(2, 4, 5)
    step(2, 6, 7, 8, 9, 10, 11)
    step(3, 2, 3)
    step(3, 4, 5)
    step(3, 6, 7, 8, 9, 10, 11)
    last_step(0, 1, 2, 3, 4, 5, 6, 7, 8, 9, 10, 11)

    for i in range(PIECES):
        far_copy(i).wait_send()
        for d in range(3 if i < NEAR else 0):
            near_copy(d, i).wait_send()
        for j in range(4 if i < NEAR else 1):
            pass_copy(j, i).wait_send()
    own_out.wait_send()
    tok_out.wait_send()
    remote(tot.at[most], tot.at[most], tsem.at[0], tsem.at[1], sib).wait_send()
    for q in range(4):
        for k in range(4):
            left(k, q)
    for q in range(5):
        g_copy(q).wait_send()
    for u in range(12):
        for k in range(3):
            halve(u, k).wait_send()
        p = part.at[UNITS[u][0], pl.ds(1, 7), :, lanes(u)]
        remote(p, p, wsem.at[u, 3], wrsem.at[u, 3], sib).wait_send()
    out_copy.wait()
    gt_copy.wait()


def settle_kernel(a, b, c, a2, b2, c2, va, vb, vc, sem):
    moves = [(a.at[0, pl.ds(64 * i, 64)], va.at[pl.ds(64 * i, 64)], a2.at[0, pl.ds(64 * i, 64)]) for i in range(4)]
    moves += [(b.at[0, pl.ds(64 * i, 64)], vb.at[pl.ds(64 * i, 64)], b2.at[0, pl.ds(64 * i, 64)]) for i in range(4)]
    moves.append((c, vc, c2))
    ins = [pltpu.make_async_copy(m[0], m[1], sem.at[0, i]) for i, m in enumerate(moves)]
    outs = [pltpu.make_async_copy(m[1], m[2], sem.at[1, i]) for i, m in enumerate(moves)]
    for m in ins:
        m.start()
    for m, n in zip(ins, outs):
        m.wait()
        n.start()
    for n in outs:
        n.wait()


def settle(*arrays):
    v = pl.BlockSpec(memory_space=pl.ANY)
    return pl.pallas_call(
        settle_kernel,
        name="settle",
        out_shape=tuple(jax.ShapeDtypeStruct(v.shape, v.dtype) for v in arrays),
        in_specs=[v] * 3,
        out_specs=(v,) * 3,
        scratch_shapes=[
            pltpu.VMEM((T, INNER), BF),
            pltpu.VMEM((T, D), BF),
            pltpu.VMEM((16, COLS), F32),
            pltpu.SemaphoreType.DMA((2, 9)),
        ],
        compiler_params=pltpu.CompilerParams(vmem_limit_bytes=60 * 1024 * 1024),
    )(*arrays)


def on_device(tokens, w_in, log_decay, grad_out):
    v = pl.BlockSpec(memory_space=pltpu.VMEM)
    a = pl.BlockSpec(memory_space=pl.ANY)
    vm = pltpu.VMEM
    st = vm((4, 2, 32, 16, N), BF)
    sr = vm((4, 32, 2, 16, N), BF)
    dma = pltpu.SemaphoreType.DMA
    out, gt, gw = pl.pallas_call(
        kernel,
        name="mixer_step",
        out_shape=(
            jax.ShapeDtypeStruct((T, INNER), BF),
            jax.ShapeDtypeStruct((T, D), BF),
            jax.ShapeDtypeStruct((16, COLS), F32),
        ),
        in_specs=[a, a, v, a],
        out_specs=(a, a, v),
        scratch_shapes=[
            vm((D, COLS), BF),
            vm((T, D), BF),
            vm((2, 64, 16, T), BF),
            vm((64, 16, T), BF),
            vm((64, 16, T), BF),
            vm((64, 16, T), BF),
            vm((T, INNER), BF),
            vm((INNER, T), BF),
            vm((COLS, T), BF),
            vm((H, 8, T), F32),
            vm((H, 8, N), F32),
            vm((H, 8, N), F32),
            vm((H, T, T), BF),
            vm((T, T), BF),
            vm((H, PS, T), F32),
            vm((H, PS, T), BF),
            vm((H, 2 * PS, T), BF),
            vm((H, 2 * PS, T), BF),
            vm((T, T), F32),
            vm((N, T), F32),
            vm((N, T), F32),
            vm((T, N), BF),
            vm((T, N), BF),
            st, sr, sr, st, st, sr, sr, st,
            vm((INNER, T), BF),
            vm((T, INNER), BF),
            vm((INNER, T), BF),
            vm((T, COLS), BF),
            vm((T, COLS), BF),
            vm((6, 32, 16, CW), BF),
            vm((6, 63, 16, CW), BF),
            vm((6, 63, 16, CW), BF),
            dma((5,)),
            dma((PIECES,)),
            dma((PIECES,)),
            dma((3, PIECES)),
            dma((3, PIECES)),
            dma((4, PIECES)),
            dma((4, PIECES)),
            dma((2,)),
            dma((2,)),
            dma((5,)),
            dma((5,)),
            dma((4, 4)),
            dma((4, 4)),
            dma((2,)),
            dma((12, 4)),
            dma((12, 4)),
        ],
        compiler_params=pltpu.CompilerParams(
            collective_id=0, has_side_effects=True, vmem_limit_bytes=60 * 1024 * 1024
        ),
    )(tokens[0], w_in, log_decay[0], grad_out[0])
    return settle(out[None], gt[None], gw)


def solution(mesh):
    return jax.shard_map(
        on_device,
        mesh=mesh,
        in_specs=(
            P("fsdp", "seq", None),
            P("fsdp", None),
            P("fsdp", None, "seq"),
            P("fsdp", "seq", None),
        ),
        out_specs=(P("fsdp", "seq", None), P("fsdp", "seq", None), P(("seq", "fsdp"), None)),
        check_vma=False,
    )
```
